32 devices in a mesh: dir: 2 (over y), row: 4 (over z), col: 4 (over x, core).
Axes of the slice: x: 2, y: 2, z: 4, core: 2. Of those that a mesh axis runs over, the one named last changes fastest.
Arguments:
- cotangent: bfloat16 [2048, 512], P('dir'), may hold values from -3 to 3
- radiation: bfloat16 [2, 8192, 2048], P(None, ('row', 'col'), 'dir'), may hold values from -0.125 to 0.125
- near_z: float32 [2, 256, 512, 512], P(None, ('dir', 'row', 'col')), may hold values from -0.25 to 0.25
- near_pairs: int32 [256, 2], P(('dir', 'row', 'col')), may hold values from 0 to 15, as said below
- far_ut: float32 [2, 128, 96, 512], P(None, ('dir', 'row', 'col')), may hold values from -0.25 to 0.25
- far_vt: float32 [2, 128, 96, 512], P(None, ('dir', 'row', 'col')), may hold values from -0.625 to 0.625
- far_pairs: int32 [128, 2], P(('dir', 'row', 'col')), may hold values from 0 to 15, as said below
- far_ranks: int32 [128], P(('dir', 'row', 'col')), may hold values from 32 to 96
- block_counts: int32 [32, 2], P(('dir', 'row', 'col')), may hold values from 1 to 8, as said below
Outputs:
- adjoint: float32 [8192, 512], P(('col', 'dir', 'row'))
The draws below stay inside these ranges and needn't reach their ends.
Inputs may be any that keep to these rules, and one draw needn't show every extreme that they name: `near_pairs`: slot s belongs to the device at position g = s div 8 in the order dir, row, col, with row index r and column index c; its row cluster lies in r * 4 to (r + 1) * 4 - 1 and its column cluster in c * 4 to (c + 1) * 4 - 1. Pairs may repeat. `far_pairs`: slot s belongs to the device at position s div 4 in the order dir, row, col, with row index r and column index c; its row cluster lies in r * 4 to (r + 1) * 4 - 1 and its column cluster in c * 4 to (c + 1) * 4 - 1. Pairs may repeat. `block_counts`: column 0 is at most 8 and column 1 at most 4; the live slots of a device are its first ones.
All inputs are finite; a program needn't handle non-finite values.
Results may differ from the reference program's by a relative error of at most 0.0003.
Values sent between devices are 32-bit elements; how exact they have to be, the bound alone decides.
A program may use at most 128 MiB of HBM per device.

```python
import jax
import jax.numpy as jnp
from jax import lax

CLUSTER = 512
RMAX = 96
RMIN = 32
RHS = 256
NEAR_DEV = 8
FAR_DEV = 4
DIRS = 2048
NU = 8192
N_ROW = 4
N_COL = 4
DEVICES = 32


def cluster_pairs(key, per_device):
    total = DEVICES * per_device
    slots = jnp.arange(total, dtype=jnp.int32)
    device_pos = slots // per_device
    row_group = device_pos // N_COL % N_ROW
    col_group = device_pos % N_COL
    first_key, second_key = jax.random.split(key)
    rows = row_group * N_COL + jax.random.randint(first_key, (total,), 0, N_COL, dtype=jnp.int32)
    cols = col_group * N_ROW + jax.random.randint(second_key, (total,), 0, N_ROW, dtype=jnp.int32)
    last_slot = (DEVICES - 1) * per_device
    rows = rows.at[0].set(0).at[last_slot].set(N_ROW * N_COL - 1)
    cols = cols.at[0].set(0).at[last_slot].set(N_ROW * N_COL - 1)
    return jnp.stack([rows, cols], axis=1).astype(jnp.int32)


def draw_near_pairs(key, part):
    return cluster_pairs(jax.random.fold_in(key, 11), NEAR_DEV)


def draw_far_pairs(key, part):
    return cluster_pairs(jax.random.fold_in(key, 23), FAR_DEV)


def draw_far_ranks(key, part):
    total = DEVICES * FAR_DEV
    ranks = jax.random.randint(jax.random.fold_in(key, 37), (total,), RMIN, RMAX + 1, dtype=jnp.int32)
    ranks = ranks.at[0].set(RMAX).at[FAR_DEV].set(RMIN)
    return ranks.astype(jnp.int32)


def skewed_counts(key, most):
    first_key, second_key = jax.random.split(key)
    chosen = jax.random.randint(first_key, (DEVICES,), 0, 4, dtype=jnp.int32)
    counts = jnp.where(chosen == 0, most, max(1, most // 4)).astype(jnp.int32)
    forced = jax.random.randint(second_key, (), 0, DEVICES, dtype=jnp.int32)
    return counts.at[forced].set(most)


def draw_block_counts(key, part):
    near_counts = skewed_counts(jax.random.fold_in(key, 41), NEAR_DEV)
    far_counts = skewed_counts(jax.random.fold_in(key, 43), FAR_DEV)
    return jnp.stack([near_counts, far_counts], axis=1).astype(jnp.int32)


def shard_levels(key, dims, cuts, smallest, largest):
    gain = 1.0
    for dim, shards_of in cuts:
        steps = jax.random.uniform(jax.random.fold_in(jax.random.fold_in(key, 6), dim), (shards_of,), jnp.float32, smallest / len(cuts), largest / len(cuts))
        gain = gain * jnp.repeat(jnp.exp(steps), dims[dim] // shards_of).reshape((-1,) + (1,) * (len(dims) - 1 - dim))
    return gain


def scatter_about(key, extent, spread, reach, shards=(), held_as=jnp.bfloat16):
    array = jax.random.normal(key, extent, jnp.float32) * spread
    if len(shards) > 0:
        array = shard_levels(key, extent, shards, -0.22, 0.18) * array
    return jnp.clip(array, min=-reach, max=reach).astype(held_as)


def setup_inputs(seed: int = 0) -> dict:
    streams_of = jax.random.split(jax.random.key(seed), 10)
    return {
        "cotangent": scatter_about(streams_of[0], (DIRS, 2 * RHS), 0.5, 3.0, ((0, 2),)),
        "radiation": scatter_about(streams_of[1], (2, NU, DIRS), DIRS ** -0.5, 0.125, ((1, 16), (2, 2))),
        "near_z": scatter_about(streams_of[2], (2, DEVICES * NEAR_DEV, CLUSTER, CLUSTER), CLUSTER ** -0.5, 0.25, ((1, 32),), jnp.float32),
        "near_pairs": draw_near_pairs(jax.random.fold_in(streams_of[9], 71), 0),
        "far_ut": scatter_about(streams_of[4], (2, DEVICES * FAR_DEV, RMAX, CLUSTER), CLUSTER ** -0.5, 0.25, ((1, 32),), jnp.float32),
        "far_vt": scatter_about(streams_of[5], (2, DEVICES * FAR_DEV, RMAX, CLUSTER), RMAX ** -0.5, 0.625, ((1, 32),), jnp.float32),
        "far_pairs": draw_far_pairs(jax.random.fold_in(streams_of[9], 71), 0),
        "far_ranks": draw_far_ranks(jax.random.fold_in(streams_of[9], 71), 0),
        "block_counts": draw_block_counts(jax.random.fold_in(streams_of[9], 71), 0),
    }


def swap_parts(values):
    half_width = values.shape[1] // 2
    return jnp.concatenate([-values[:, half_width:], values[:, :half_width]], axis=1)


def transposed_dot(left, right):
    return lax.dot_general(left, right, (((0,), (0,)), ((), ())), precision=lax.Precision.HIGHEST, preferred_element_type=jnp.float32)


def plain_dot(left, right):
    return jnp.dot(left, right, precision=lax.Precision.HIGHEST, preferred_element_type=jnp.float32)


def add_rows(total, term, start):
    current = lax.dynamic_slice_in_dim(total, start, term.shape[0], 0)
    return lax.dynamic_update_slice_in_dim(total, current + term, start, 0)


def reference(cotangent, radiation, near_z, near_pairs, far_ut, far_vt, far_pairs, far_ranks, block_counts):
    rhs_full = jnp.dot(radiation[0], cotangent, preferred_element_type=jnp.float32) + jnp.dot(radiation[1], swap_parts(cotangent), preferred_element_type=jnp.float32)
    rhs_swap = swap_parts(rhs_full)
    rank_most = far_ut.shape[2]

    def near_step(slot_index, total):
        slot_index = jnp.asarray(slot_index).astype(jnp.int32)
        device_pos = slot_index // NEAR_DEV
        live = (slot_index % NEAR_DEV) < block_counts[device_pos, 0]

        def apply_block(total):
            row_start = (near_pairs[slot_index, 0] * CLUSTER).astype(jnp.int32)
            col_start = (near_pairs[slot_index, 1] * CLUSTER).astype(jnp.int32)
            source = lax.dynamic_slice_in_dim(rhs_full, row_start, CLUSTER, 0)
            source_swap = lax.dynamic_slice_in_dim(rhs_swap, row_start, CLUSTER, 0)
            blocks = near_z[:, slot_index]
            term = transposed_dot(blocks[0], source) + transposed_dot(blocks[1], source_swap)
            return add_rows(total, term, col_start)

        return lax.cond(live, apply_block, lambda kept: kept, total)

    def far_step(slot_index, total):
        slot_index = jnp.asarray(slot_index).astype(jnp.int32)
        device_pos = slot_index // FAR_DEV
        live = (slot_index % FAR_DEV) < block_counts[device_pos, 1]

        def apply_block(total):
            row_start = (far_pairs[slot_index, 0] * CLUSTER).astype(jnp.int32)
            col_start = (far_pairs[slot_index, 1] * CLUSTER).astype(jnp.int32)
            source = lax.dynamic_slice_in_dim(rhs_full, row_start, CLUSTER, 0)
            source_swap = lax.dynamic_slice_in_dim(rhs_swap, row_start, CLUSTER, 0)
            left_f = far_ut[:, slot_index]
            right_f = far_vt[:, slot_index]
            coeffs = plain_dot(left_f[0], source) + plain_dot(left_f[1], source_swap)
            keep_rows = (lax.iota(jnp.int32, rank_most) < far_ranks[slot_index])[:, None]
            coeffs = jnp.where(keep_rows, coeffs, jnp.zeros_like(coeffs))
            term = transposed_dot(right_f[0], coeffs) + transposed_dot(right_f[1], swap_parts(coeffs))
            return add_rows(total, term, col_start)

        return lax.cond(live, apply_block, lambda kept: kept, total)

    total = jnp.zeros(rhs_full.shape, jnp.float32)
    total = lax.fori_loop(0, near_pairs.shape[0], near_step, total)
    total = lax.fori_loop(0, far_pairs.shape[0], far_step, total)
    return total
```

```python
import functools

import jax
import jax.numpy as jnp
from jax import lax
from jax.experimental import pallas as pl
from jax.experimental.pallas import tpu as pltpu
from jax.sharding import PartitionSpec as P

CORES = 2
MESH = pl.DeviceIdType.MESH
F32 = jnp.float32
BF16 = jnp.bfloat16
NT = (((1,), (1,)), ((), ()))
PARTS = 8
SIZES = (1, 1, 2, 2, 2)
ROW_FIRST = (1.0, 0.0, 0.5, 0.0, 0.0)


def dot(left, right):
    return jnp.dot(left, right, preferred_element_type=F32)


def dot_nt(left, right):
    return lax.dot_general(left, right, NT, preferred_element_type=F32)


def split(values):
    high = values.astype(BF16)
    return high, (values - high.astype(F32)).astype(BF16)


def swap_rows(values):
    half = values.shape[0] // 2
    return jnp.concatenate([-values[half:], values[:half]], axis=0)


def fold(values):
    half = values.shape[0] // 2
    return values[:half] + values[half:]


class Plan:
    def __init__(self, wide, n_row):
        unit = wide // 2 // PARTS
        self.half = [unit * size for size in SIZES]
        self.width = [2 * half for half in self.half]
        self.first = [sum(self.half[:k]) for k in range(len(self.half))]
        self.row_wide = [int(width * share) for width, share in zip(self.width, ROW_FIRST)]
        self.row_at = [sum(self.row_wide[:k]) for k in range(len(self.half))]
        self.row_total = max(8, sum(self.row_wide))
        self.chunks = len(self.half)
        self.offsets = sorted(range(1, n_row), key=lambda o: -min(o, n_row - o)) + [0]

    def rows(self, k):
        return slice(2 * self.first[k], 2 * self.first[k] + self.width[k])

    def dir_rows(self, k):
        start = 2 * self.first[k]
        return slice(start, start + self.width[k] - self.row_wide[k])

    def row_rows(self, k):
        stop = 2 * self.first[k] + self.width[k]
        return slice(stop - self.row_wide[k], stop)

    def row_slots(self, k):
        return slice(self.row_at[k], self.row_at[k] + self.row_wide[k])


def kernel(
    n_dir, n_row, n_col, plan,
    near_pairs, far_pairs, far_ranks, counts, cot_hbm, rad_hbm, near_z, far_ut, far_vt,
    out,
    placed, cot, rad, z_high, z_low, stage, far_stage, left_far, right_far, cot_t, totals, sent, dir_in, gathered, sides, terms,
    parts, dir_parts, row_parts, pair_in, row_in, last_in,
    in_sem, stage_sem, far_sem, d_send, d_recv, x_send, x_recv, c_send, c_recv, p_send, p_recv, r_send, r_recv,
    a_recv, q_send, q_recv, l_send, l_recv, o_sem,
):
    chunks = plan.chunks
    wide = cot.shape[1]
    stages = stage.shape[0]
    rank_most, rank_pad = far_ut.shape[2], left_far.shape[2] // 2
    n_near, n_far = near_z.shape[1], far_ut.shape[1]
    block = near_z.shape[2]
    piece = block // n_dir
    n_x = n_col // CORES
    per_dir = n_row // n_dir
    n_off = len(plan.offsets)
    d = lax.axis_index("dir")
    r = lax.axis_index("row")
    c = lax.axis_index("col")
    x, core = c // CORES, c % CORES
    partner = x * CORES + (CORES - 1 - core)
    row_pair = r + 1 - 2 * lax.rem(r, 2)

    def dir_peer(j):
        return (lax.rem(d + j, n_dir), r, c)

    def x_peer(j):
        return (d, r, lax.rem(x + j, n_x) * CORES + core)

    def row_peer(i):
        return (d, lax.rem(r + plan.offsets[i], n_row), c)

    def from_x(j, core_of):
        return lax.rem(x + n_x - j, n_x) * CORES + core_of

    def remote(src, dst, send, recv, device):
        return pltpu.make_async_remote_copy(
            src_ref=src, dst_ref=dst, send_sem=send, recv_sem=recv, device_id=device, device_id_type=MESH
        )

    peers = [dir_peer(j) for j in range(1, n_dir)]
    peers += [x_peer(j) for j in range(1, n_x)]
    peers += [row_peer(i) for i in range(n_off - 1)]
    peers.append((d, r, partner))
    barrier = pltpu.get_barrier_semaphore()
    for device in peers:
        pl.semaphore_signal(barrier, inc=1, device_id=device, device_id_type=MESH)

    inputs = [pltpu.make_async_copy(cot_hbm, cot, in_sem.at[0])]
    inputs += [pltpu.make_async_copy(rad_hbm.at[part], rad.at[part], in_sem.at[1 + part]) for part in range(2)]
    for load in inputs:
        load.start()

    def load_item(item):
        slot, part = item // 2, lax.rem(item, 2)
        return pltpu.make_async_copy(
            near_z.at[part, slot], stage.at[lax.rem(item, stages)], stage_sem.at[lax.rem(item, stages)]
        )

    def load_far(s):
        side = lax.rem(s, 2)
        return [
            pltpu.make_async_copy(source.at[part, s], far_stage.at[side, 2 * i + part], far_sem.at[side, 2 * i + part])
            for i, source in enumerate((far_ut, far_vt))
            for part in range(2)
        ]

    def send_dir(k, j):
        rows = plan.rows(k)
        return remote(sent.at[rows], dir_in.at[j - 1, rows], d_send.at[k, j - 1], d_recv.at[k, j - 1], dir_peer(j))

    def send_x(k, j, which=None):
        block_of = gathered.at[c if which is None else which, plan.rows(k)]
        return remote(block_of, block_of, x_send.at[k, j - 1], x_recv.at[k, j - 1], x_peer(j))

    def send_core(k, j, core_of):
        block_of = gathered.at[from_x(j, core_of), plan.rows(k)]
        return remote(block_of, block_of, c_send.at[k, j], c_recv.at[k, j], (d, r, partner))

    def send_part(k, j, i):
        rows = plan.dir_rows(k)
        return remote(
            parts.at[j, i, rows], dir_parts.at[j - 1, i, rows], p_send.at[k, j - 1, i], p_recv.at[k, j - 1, i], dir_peer(j)
        )

    def send_row(k, i):
        rows = plan.dir_rows(k)
        return remote(parts.at[0, i, rows], row_parts.at[i, rows], r_send.at[k, i], r_recv.at[k, i], row_peer(i))

    def row_of(i):
        return lax.rem(r + plan.offsets[i], n_row)

    def same_pair(i):
        return row_of(i) // 2 == r // 2

    def gathers(i):
        above = row_of(i) > r
        odd = lax.rem(r, 2) == 1
        return jnp.logical_not(same_pair(i)) & (above == odd)

    def send_pair(k, i, j):
        return remote(
            parts.at[j, i, plan.row_rows(k)],
            pair_in.at[row_of(i), j, plan.row_slots(k)],
            q_send.at[k, i, j],
            a_recv.at[k, row_of(i), j],
            (d, row_pair, c),
        )

    def send_sum(k, i, j):
        return remote(
            parts.at[j, i, plan.row_rows(k)],
            row_in.at[r // 2, j, plan.row_slots(k)],
            q_send.at[k, i, j],
            q_recv.at[k, r // 2, j],
            row_peer(i),
        )

    def send_last(k, j):
        return remote(
            parts.at[j, n_off - 1, plan.row_rows(k)],
            last_in.at[j - 1, plan.row_slots(k)],
            l_send.at[k, j - 1],
            l_recv.at[k, j - 1],
            dir_peer(j),
        )

    def right_sides(k):
        at, half = plan.first[k], plan.half[k]
        left = jnp.concatenate([cot_t[at : at + half], cot_t[wide // 2 + at : wide // 2 + at + half]], axis=0)
        sent[plan.rows(k)] = dot_nt(left, rad[0]) + dot_nt(swap_rows(left), rad[1])

    def convert(first, last):
        def body(item, carry):
            load_item(item).wait()
            high, low = split(stage[lax.rem(item, stages)])
            rows = pl.ds(pl.multiple_of(lax.rem(item, 2) * block, block), block)
            z_high[item // 2, rows, :] = high
            z_low[item // 2, rows, :] = low

            @pl.when(item + stages < 2 * n_near)
            def _():
                load_item(item + stages).start()

            return carry

        lax.fori_loop(2 * first, 2 * last, body, 0)

    def pack_far():
        rest = jnp.zeros((rank_pad - rank_most, block), F32)

        def body(s, carry):
            for load in load_far(s):
                load.wait()
            side = lax.rem(s, 2)
            for part in range(2):
                factor = jnp.concatenate([far_stage[side, part], rest], axis=0)
                high, low = split(factor.T)
                rows = slice(part * block, (part + 1) * block)
                left_far[s, rows, :rank_pad] = high
                left_far[s, rows, rank_pad:] = low
                factor = jnp.concatenate([far_stage[side, 2 + part], rest], axis=0)
                high, low = split(factor)
                rows = slice(part * rank_pad, (part + 1) * rank_pad)
                right_far[0, s, rows, :] = high
                right_far[1, s, rows, :] = low

            @pl.when(s + 2 < n_far)
            def _():
                for load in load_far(s + 2):
                    load.start()

            return carry

        lax.fori_loop(0, n_far, body, 0)

    def add_dirs(k):
        rows = plan.rows(k)
        for j in range(1, n_dir):
            send_dir(k, j).wait_recv()
        total = sent[rows]
        for j in range(1, n_dir):
            total = total + dir_in[j - 1, rows]
        gathered[c, rows] = total
        for j in range(1, n_x):
            send_x(k, j).start()
        send_core(k, 0, core).start()

    def relay(k):
        for j in range(1, n_x):
            send_x(k, j, from_x(j, core)).wait_recv()
            send_core(k, j, core).start()

    def products(k, between=None):
        between = {min(stop, n_far): calls for stop, calls in (between or {}).items()}
        width, rows = plan.width[k], plan.rows(k)
        for j in range(n_x):
            send_core(k, j, CORES - 1 - core).wait_recv()

        def side(q, carry):
            values = gathered[q, rows]
            high, low = split(jnp.concatenate([values, swap_rows(values)], axis=1))
            sides[q, :width] = high
            sides[q, width : 2 * width] = low
            return carry

        lax.fori_loop(0, n_col, side, 0)

        per_far = n_near // n_far

        def near(s):
            left = sides[lax.rem(near_pairs[0, s], n_col), : 2 * width]
            terms[s, :width] = fold(dot(left, z_high[s])) + dot(left[:width], z_low[s])

        def body(s, carry):
            both = dot(sides[lax.rem(far_pairs[0, s], n_col), : 2 * width], left_far[s])
            near(s * per_far)
            coeffs = fold(both[:, :rank_pad]) + both[:width, rank_pad:]
            lanes = lax.broadcasted_iota(jnp.int32, coeffs.shape, 1)
            coeffs = jnp.where(lanes < far_ranks[s], coeffs, 0.0)
            high, low = split(jnp.concatenate([coeffs, swap_rows(coeffs)], axis=1))
            for i in range(1, per_far):
                near(s * per_far + i)
            both = dot(jnp.concatenate([high, low], axis=0), right_far[0, s])
            terms[n_near + s, :width] = fold(both) + dot(high, right_far[1, s])
            return carry

        at = 0
        for stop in sorted({*between, n_far}):
            if stop > at:
                lax.fori_loop(at, stop, body, 0)
            at = stop
            for call, i in between.pop(stop, ()):
                call(i)

        for j in list(range(1, n_dir)) + [0]:
            for i in range(n_off):
                q = row_of(i)
                target = c * n_row + lax.rem(d + j, n_dir) * per_dir + q // n_dir
                lanes = pl.ds(pl.multiple_of(lax.rem(q, n_dir) * piece, piece), piece)
                gains = [
                    jnp.where((near_pairs[1, s] == target) & (s < counts[0, 0]), 1.0, 0.0) for s in range(n_near)
                ] + [jnp.where((far_pairs[1, s] == target) & (s < counts[0, 1]), 1.0, 0.0) for s in range(n_far)]
                total = terms[0, :width, lanes] * gains[0]
                for s in range(1, n_near + n_far):
                    total = total + terms[s, :width, lanes] * gains[s]
                parts[j, i, rows] = total
                if j > 0 and plan.row_wide[k] < width:
                    send_part(k, j, i).start()
                if i < n_off - 1 and plan.row_wide[k] > 0:
                    own = same_pair(i)
                    mine = gathers(i)

                    @pl.when(own)
                    def _():
                        send_sum(k, i, j).start()

                    @pl.when(jnp.logical_not(own | mine))
                    def _():
                        send_pair(k, i, j).start()

    def add_parts(k, first=0, last=n_off):
        if plan.row_wide[k] == plan.width[k]:
            return
        rows = plan.dir_rows(k)
        for i in range(first, last):
            total = parts[0, i, rows]
            for j in range(1, n_dir):
                send_part(k, j, i).wait_recv()
                total = total + dir_parts[j - 1, i, rows]
            parts[0, i, rows] = total
            if i < n_off - 1:
                send_row(k, i).start()

    def add_pairs(k):
        if plan.row_wide[k] == 0:
            return
        rows, slots = plan.row_rows(k), plan.row_slots(k)
        for j in list(range(1, n_dir)) + [0]:
            for i in range(n_off - 1):

                @pl.when(gathers(i))
                def _():
                    send_pair(k, i, j).wait_recv()
                    parts[j, i, rows] = parts[j, i, rows] + pair_in[row_of(i), j, slots]
                    send_sum(k, i, j).start()

    def add_rows(k):
        if plan.row_wide[k] == 0:
            return
        rows, slots = plan.row_rows(k), plan.row_slots(k)
        for j in list(range(1, n_dir)) + [0]:
            total = parts[j, n_off - 1, rows]
            for p in range(n_row // 2):
                remote(
                    parts.at[j, n_off - 1, rows], row_in.at[p, j, slots], l_send.at[k, 0], q_recv.at[k, p, j], row_peer(0)
                ).wait_recv()
                total = total + row_in[p, j, slots]
            parts[j, n_off - 1, rows] = total
            if j > 0:
                send_last(k, j).start()

    def place(k, start, total):
        half, at = plan.half[k], plan.first[k]
        stop = start + total.shape[0]
        if start < half:
            cut = min(stop, half)
            totals[at + start : at + cut] = total[: cut - start]
        if stop > half:
            cut = max(start, half)
            base = wide // 2 + at - half
            totals[base + cut : base + stop] = total[cut - start :]

    def finish_dir(k):
        if plan.row_wide[k] == plan.width[k]:
            return
        rows = plan.dir_rows(k)
        total = parts[0, n_off - 1, rows]
        for i in range(n_off - 1):
            send_row(k, i).wait_recv()
            total = total + row_parts[i, rows]
        place(k, 0, total)

    def finish_row(k):
        if plan.row_wide[k] == 0:
            return
        rows, slots = plan.row_rows(k), plan.row_slots(k)
        total = parts[0, n_off - 1, rows]
        for j in range(1, n_dir):
            send_last(k, j).wait_recv()
            total = total + last_in[j - 1, slots]
        place(k, plan.width[k] - plan.row_wide[k], total)

    def put(first, last):
        for base in (0, wide // 2):
            columns = slice(base + first, base + last)
            placed[:, columns] = totals[columns].T
            copy = pltpu.make_async_copy(placed.at[:, columns], out.at[:, columns], o_sem.at[len(put_copies)])
            copy.start()
            put_copies.append(copy)

    def drain():
        for k in range(chunks):
            for j in range(1, n_dir):
                send_dir(k, j).wait_send()
            for j in range(1, n_x):
                send_x(k, j).wait_send()
            for j in range(n_x):
                send_core(k, j, core).wait_send()
            if plan.row_wide[k] < plan.width[k]:
                for i in range(n_off):
                    for j in range(1, n_dir):
                        send_part(k, j, i).wait_send()
                    if i < n_off - 1:
                        send_row(k, i).wait_send()
            if plan.row_wide[k] > 0:
                for j in range(n_dir):
                    for i in range(n_off - 1):
                        send_sum(k, i, j).wait_send()
                    if j > 0:
                        send_last(k, j).wait_send()
        for copy in put_copies:
            copy.wait()

    put_copies = []

    for load in inputs:
        load.wait()
    for item in range(stages):
        load_item(item).start()
    for s in range(min(2, n_far)):
        for load in load_far(s):
            load.start()
    cot_t[...] = cot[...].T
    for k in range(chunks):
        right_sides(k)
        if k == 1:
            pl.semaphore_wait(barrier, len(peers))
        for i in ((0, 1) if k == 1 else (k,) if k > 1 else ()):
            for j in range(1, n_dir):
                send_dir(i, j).start()

    convert(0, n_near)
    add_dirs(0)
    pack_far()
    add_dirs(1)
    relay(0)
    products(0, {2: [(relay, 1), (add_dirs, 2)]})
    products(1, {2: [(add_dirs, 3)], 4: [(relay, 2)]})
    products(2, {1: [(add_pairs, 0)], 2: [(add_dirs, 4)], 4: [(relay, 3)]})
    products(3, {1: [(add_rows, 0)], 2: [(add_parts, 1)], 4: [(relay, 4)]})
    products(4, {1: [(add_pairs, 2)], 3: [(add_parts, 2)]})
    add_rows(2)
    finish_row(0)
    finish_dir(1)
    add_parts(3)
    finish_dir(2)
    add_parts(4)
    finish_row(2)
    put(0, plan.first[3])
    finish_dir(3)
    finish_dir(4)
    put(plan.first[3], wide // 2)
    drain()


def shards(
    cotangent, radiation, near_z, near_pairs, far_ut, far_vt, far_pairs, far_ranks, block_counts
):
    n_dir, n_row, n_col = (lax.axis_size(name) for name in ("dir", "row", "col"))
    deep, wide = cotangent.shape
    plan = Plan(wide, n_row)
    chunks, most = plan.chunks, max(plan.width)
    block = near_z.shape[2]
    n_near, n_far, rank_most = near_z.shape[1], far_ut.shape[1], far_ut.shape[2]
    n_x = n_col // CORES
    piece = block // n_dir
    small = n_row * n_col <= 16
    stages = min(6 if small else 2, 2 * n_near)
    rank_pad = -(-rank_most // 128) * 128
    smem = pl.BlockSpec(memory_space=pltpu.SMEM)
    anywhere = pl.BlockSpec(memory_space=pl.ANY)
    dma = pltpu.SemaphoreType.DMA
    return pl.pallas_call(
        functools.partial(kernel, n_dir, n_row, n_col, plan),
        out_shape=jax.ShapeDtypeStruct((piece, wide), F32),
        in_specs=[smem] * 4 + [anywhere] * 5,
        out_specs=anywhere,
        scratch_shapes=[
            pltpu.VMEM((piece, wide), F32),
            pltpu.VMEM((deep, wide), BF16),
            pltpu.VMEM(radiation.shape, BF16),
            pltpu.VMEM((n_near, 2 * block, block), BF16),
            pltpu.VMEM((n_near, 2 * block, block), BF16),
            pltpu.VMEM((stages, block, block), F32),
            pltpu.VMEM((2, 4, rank_most, block), F32),
            pltpu.VMEM((n_far, 2 * block, 2 * rank_pad), BF16),
            pltpu.VMEM((2, n_far, 2 * rank_pad, block), BF16),
            pltpu.VMEM((wide, deep), BF16),
            pltpu.VMEM((wide, piece), F32),
            pltpu.VMEM((wide, block), F32),
            pltpu.VMEM((n_dir - 1, wide, block), F32),
            pltpu.VMEM((n_col, wide, block), F32),
            pltpu.VMEM((n_col, 2 * most, 2 * block), BF16),
            pltpu.VMEM((n_near + n_far, most, block), F32),
            pltpu.VMEM((n_dir, n_row, wide, piece), F32),
            pltpu.VMEM((n_dir - 1, n_row, wide, piece), F32),
            pltpu.VMEM((n_row - 1, wide, piece), F32),
            pltpu.VMEM((n_row, n_dir, plan.row_total, piece), F32),
            pltpu.VMEM((n_row // 2, n_dir, plan.row_total, piece), F32),
            pltpu.VMEM((n_dir - 1, plan.row_total, piece), F32),
            dma((3,)),
            dma((stages,)),
            dma((2, 4)),
            dma((chunks, n_dir - 1)),
            dma((chunks, n_dir - 1)),
            dma((chunks, n_x - 1)),
            dma((chunks, n_x - 1)),
            dma((chunks, n_x)),
            dma((chunks, n_x)),
            dma((chunks, n_dir - 1, n_row)),
            dma((chunks, n_dir - 1, n_row)),
            dma((chunks, n_row)),
            dma((chunks, n_row)),
            dma((chunks, n_row, n_dir)),
            dma((chunks, n_row, n_dir)),
            dma((chunks, n_row // 2, n_dir)),
            dma((chunks, n_dir - 1)),
            dma((chunks, n_dir - 1)),
            dma((4,)),
        ],
        compiler_params=pltpu.CompilerParams(
            collective_id=0, has_side_effects=True, vmem_limit_bytes=67043328
        ),
    )(near_pairs.T, far_pairs.T, far_ranks, block_counts, cotangent, radiation, near_z, far_ut, far_vt)


def solution(mesh):
    return jax.shard_map(
        shards,
        mesh=mesh,
        in_specs=(
            P("dir", None),
            P(None, ("row", "col"), "dir"),
            P(None, ("dir", "row", "col"), None, None),
            P(("dir", "row", "col"), None),
            P(None, ("dir", "row", "col"), None, None),
            P(None, ("dir", "row", "col"), None, None),
            P(("dir", "row", "col"), None),
            P(("dir", "row", "col")),
            P(("dir", "row", "col"), None),
        ),
        out_specs=P(("col", "dir", "row"), None),
        check_vma=False,
    )
```

```python
import functools

import jax
import jax.numpy as jnp
from jax import lax
from jax.experimental import pallas as pl
from jax.experimental.pallas import tpu as pltpu
from jax.sharding import PartitionSpec as P

CORES = 2
MESH = pl.DeviceIdType.MESH
F32 = jnp.float32
BF16 = jnp.bfloat16
NT = (((1,), (1,)), ((), ()))
PARTS = 8
SIZES = (1, 1, 2, 2, 2)
ROW_FIRST = (0.875, 0.5, 0.5, 0, 0.125)
STEPS = 4
ORDER = (
    ("convert", 0), ("convert", 1), ("dirs", 0), ("convert", 2), ("convert", 3), ("pack",), ("dirs", 1), ("relay", 0),
    ("sides", 0), ("near", 0, 0), ("near", 0, 1), ("near", 0, 2), ("dirs", 2), ("relay", 1), ("near", 0, 3),
    ("sums", 0), ("sides", 1), ("near", 1, 0), ("near", 1, 1), ("near", 1, 2), ("dirs", 3), ("near", 1, 3),
    ("sums", 1), ("relay", 2), ("pairs", 0), ("sides", 2), ("near", 2, 0), ("near", 2, 1), ("dirs", 4),
    ("part", 0, 0), ("part", 0, 1), ("part", 0, 2), ("part", 0, 3), ("near", 2, 2), ("relay", 3), ("part", 1, 0),
    ("part", 1, 1), ("near", 2, 3), ("pairs", 1), ("part", 1, 2), ("far", 0, 0), ("far", 0, 1), ("part", 1, 3),
    ("sums", 2), ("rows", 0), ("far", 1, 0), ("sides", 3), ("far", 1, 1), ("near", 3, 0), ("near", 3, 1),
    ("part", 2, 0), ("near", 3, 2), ("relay", 4), ("rows", 1), ("part", 2, 1), ("near", 3, 3), ("part", 2, 2),
    ("sums", 3), ("part", 2, 3), ("sides", 4), ("near", 4, 0), ("near", 4, 1), ("pairs", 2), ("near", 4, 2),
    ("near", 4, 3), ("part", 3, 0), ("far", 2, 0), ("sums", 4), ("far", 2, 1), ("last", 0), ("end", 0), ("last", 1),
    ("end", 1), ("part", 3, 1), ("rows", 2), ("part", 3, 2), ("far", 3, 0), ("pairs", 4), ("last", 2), ("part", 3, 3),
    ("far", 3, 1), ("part", 4, 0), ("part", 4, 1), ("rows", 4), ("last", 3), ("part", 4, 2), ("far", 4, 0),
    ("part", 4, 3), ("far", 4, 1), ("end", 2), ("end", 4), ("last", 4),
)


def dot(left, right):
    return jnp.dot(left, right, preferred_element_type=F32)


def dot_nt(left, right):
    return lax.dot_general(left, right, NT, preferred_element_type=F32)


def split(values):
    high = values.astype(BF16)
    return high, (values - high.astype(F32)).astype(BF16)


def swap_rows(values):
    half = values.shape[0] // 2
    return jnp.concatenate([-values[half:], values[:half]], axis=0)


def fold(values):
    half = values.shape[0] // 2
    return values[:half] + values[half:]


class Plan:
    def __init__(self, wide, small):
        unit = wide // 2 // PARTS
        self.half = [unit * size for size in SIZES]
        self.width = [2 * half for half in self.half]
        self.first = [sum(self.half[:k]) for k in range(len(self.half))]
        self.row_wide = [int(width * share) for width, share in zip(self.width, ROW_FIRST)]
        if not small:
            self.row_wide = [min(8, rows) for rows in self.row_wide]
        self.row_at = [sum(self.row_wide[:k]) for k in range(len(self.half))]
        self.row_total = max(8, sum(self.row_wide))
        self.dir_total = sum(self.width) - sum(self.row_wide)
        self.chunks = len(self.half)

    def rows(self, k):
        return slice(2 * self.first[k], 2 * self.first[k] + self.width[k])

    def dir_rows(self, k):
        start = 2 * self.first[k]
        return slice(start, start + self.width[k] - self.row_wide[k])

    def row_rows(self, k):
        stop = 2 * self.first[k] + self.width[k]
        return slice(stop - self.row_wide[k], stop)

    def row_slots(self, k):
        return slice(self.row_at[k], self.row_at[k] + self.row_wide[k])


def kernel(
    n_dir, n_row, n_col, plan,
    near_pairs, far_pairs, far_ranks, counts, cot_hbm, rad_hbm, near_z, far_ut, far_vt,
    out,
    placed, cot, rad, z_high, z_low, stage, far_stage, left_far, right_far, cot_t, totals, sent, dir_in, gathered, sides, terms,
    parts, dir_parts, pair_dir, row_dir, pair_in, row_in, last_in,
    in_sem, stage_sem, far_sem, d_send, d_recv, x_send, x_recv, c_send, c_recv, p_send, p_recv, r_send, f_recv, r_recv,
    q_send, a_recv, q_recv, l_send, l_recv, o_sem,
):
    chunks = plan.chunks
    wide = cot.shape[1]
    stages = stage.shape[0]
    rank_most, rank_pad = far_ut.shape[2], left_far.shape[2] // 2
    n_near, n_far = near_z.shape[1], far_ut.shape[1]
    block = near_z.shape[2]
    piece = block // n_dir
    n_x = n_col // CORES
    per_dir = n_row // n_dir
    n_cross, own = n_row - 2, n_row - 1
    d = lax.axis_index("dir")
    r = lax.axis_index("row")
    c = lax.axis_index("col")
    x, core = c // CORES, c % CORES
    partner = x * CORES + (CORES - 1 - core)
    row_pair = r + 1 - 2 * lax.rem(r, 2)

    def dir_peer(j):
        return (lax.rem(d + j, n_dir), r, c)

    def x_peer(j):
        return (d, r, lax.rem(x + j, n_x) * CORES + core)

    def row_of(i):
        base = 2 * (r // 2)
        if i < n_cross:
            return jnp.where(r < n_row // 2, lax.rem(base + n_row - 1 - i, n_row), lax.rem(base + 2 + i, n_row))
        return row_pair if i == n_cross else r

    def row_peer(i):
        return (d, row_of(i), c)

    def gathers(i):
        return (row_of(i) > r) == (lax.rem(r, 2) == 1)

    def from_x(j, core_of):
        return lax.rem(x + n_x - j, n_x) * CORES + core_of

    def remote(src, dst, send, recv, device):
        return pltpu.make_async_remote_copy(
            src_ref=src, dst_ref=dst, send_sem=send, recv_sem=recv, device_id=device, device_id_type=MESH
        )

    peers = [dir_peer(j) for j in range(1, n_dir)]
    peers += [x_peer(j) for j in range(1, n_x)]
    peers += [row_peer(i) for i in range(own)]
    peers.append((d, r, partner))
    barrier = pltpu.get_barrier_semaphore()
    for device in peers:
        pl.semaphore_signal(barrier, inc=1, device_id=device, device_id_type=MESH)

    inputs = [pltpu.make_async_copy(cot_hbm, cot, in_sem.at[0])]
    inputs += [pltpu.make_async_copy(rad_hbm.at[part], rad.at[part], in_sem.at[1 + part]) for part in range(2)]
    for load in inputs:
        load.start()

    def load_item(item):
        slot, part = item // 2, lax.rem(item, 2)
        return pltpu.make_async_copy(
            near_z.at[part, slot], stage.at[lax.rem(item, stages)], stage_sem.at[lax.rem(item, stages)]
        )

    def load_far(s):
        side = lax.rem(s, 2)
        return [
            pltpu.make_async_copy(source.at[part, s], far_stage.at[side, 2 * i + part], far_sem.at[side, 2 * i + part])
            for i, source in enumerate((far_ut, far_vt))
            for part in range(2)
        ]

    def send_dir(k, j):
        rows = plan.rows(k)
        return remote(sent.at[rows], dir_in.at[j - 1, rows], d_send.at[j - 1], d_recv.at[k, j - 1], dir_peer(j))

    def send_x(k, j, which=None):
        block_of = gathered.at[c if which is None else which, plan.rows(k)]
        return remote(block_of, block_of, x_send.at[j - 1], x_recv.at[k, j - 1], x_peer(j))

    def send_core(k, j, core_of):
        block_of = gathered.at[from_x(j, core_of), plan.rows(k)]
        return remote(block_of, block_of, c_send.at[0], c_recv.at[k, j], (d, r, partner))

    def send_part(k, j, i):
        rows = plan.dir_rows(k)
        return remote(
            parts.at[j, i, rows], dir_parts.at[j - 1, i, rows], p_send.at[0], p_recv.at[k, j - 1, i], dir_peer(j)
        )

    def pair_part(k, i):
        rows = plan.dir_rows(k)
        return remote(parts.at[0, i, rows], pair_dir.at[i, rows], r_send.at[0], f_recv.at[k, i], row_peer(n_cross))

    def send_row(k, i, p):
        rows = plan.dir_rows(k)
        return remote(parts.at[0, i, rows], row_dir.at[p, rows], r_send.at[0], r_recv.at[k, p], row_peer(i))

    def send_pair(k, i, j):
        return remote(
            parts.at[j, i, plan.row_rows(k)],
            pair_in.at[i, j, plan.row_slots(k)],
            q_send.at[0],
            a_recv.at[k, i],
            row_peer(n_cross),
        )

    def send_sum(k, i, j):
        return remote(
            parts.at[j, i, plan.row_rows(k)],
            row_in.at[r // 2, j, plan.row_slots(k)],
            q_send.at[0],
            q_recv.at[k, r // 2],
            row_peer(i),
        )

    def send_last(k, j):
        return remote(
            parts.at[j, own, plan.row_rows(k)],
            last_in.at[j - 1, plan.row_slots(k)],
            l_send.at[0],
            l_recv.at[k, j - 1],
            dir_peer(j),
        )

    def right_sides(k):
        at, half = plan.first[k], plan.half[k]
        left = jnp.concatenate([cot_t[at : at + half], cot_t[wide // 2 + at : wide // 2 + at + half]], axis=0)
        sent[plan.rows(k)] = dot_nt(left, rad[0]) + dot_nt(swap_rows(left), rad[1])

    def convert(first, last):
        def body(item, carry):
            load_item(item).wait()
            high, low = split(stage[lax.rem(item, stages)])
            rows = pl.ds(pl.multiple_of(lax.rem(item, 2) * block, block), block)
            z_high[item // 2, rows, :] = high
            z_low[item // 2, rows, :] = low

            @pl.when(item + stages < 2 * n_near)
            def _():
                load_item(item + stages).start()

            return carry

        lax.fori_loop(2 * first, 2 * last, body, 0)

    def pack_far():
        rest = jnp.zeros((rank_pad - rank_most, block), F32)

        def body(s, carry):
            for load in load_far(s):
                load.wait()
            side = lax.rem(s, 2)
            for part in range(2):
                factor = jnp.concatenate([far_stage[side, part], rest], axis=0)
                high, low = split(factor.T)
                rows = slice(part * block, (part + 1) * block)
                left_far[s, rows, :rank_pad] = high
                left_far[s, rows, rank_pad:] = low
                factor = jnp.concatenate([far_stage[side, 2 + part], rest], axis=0)
                high, low = split(factor)
                rows = slice(part * rank_pad, (part + 1) * rank_pad)
                right_far[0, s, rows, :] = high
                right_far[1, s, rows, :] = low

            @pl.when(s + 2 < n_far)
            def _():
                for load in load_far(s + 2):
                    load.start()

            return carry

        lax.fori_loop(0, n_far, body, 0)

    def add_dirs(k):
        rows = plan.rows(k)
        for j in range(1, n_dir):
            send_dir(k, j).wait_recv()
        total = sent[rows]
        for j in range(1, n_dir):
            total = total + dir_in[j - 1, rows]
        gathered[c, rows] = total
        for j in range(1, n_x):
            send_x(k, j).start()
        send_core(k, 0, core).start()

    def relay(k):
        for j in range(1, n_x):
            send_x(k, j, from_x(j, core)).wait_recv()
            send_core(k, j, core).start()

    per_far = n_near // n_far

    def make_sides(k):
        width, rows = plan.width[k], plan.rows(k)
        for j in range(n_x):
            send_core(k, j, CORES - 1 - core).wait_recv()

        def side(q, carry):
            values = gathered[q, rows]
            high, low = split(jnp.concatenate([values, swap_rows(values)], axis=1))
            sides[q, :width] = high
            sides[q, width : 2 * width] = low
            return carry

        lax.fori_loop(0, n_col, side, 0)

    def multiply(k, step):
        width = plan.width[k]

        def near(s):
            left = sides[lax.rem(near_pairs[0, s], n_col), : 2 * width]
            terms[s, :width] = fold(dot(left, z_high[s])) + dot(left[:width], z_low[s])

        def body(s):
            both = dot(sides[lax.rem(far_pairs[0, s], n_col), : 2 * width], left_far[s])
            near(s * per_far)
            coeffs = fold(both[:, :rank_pad]) + both[:width, rank_pad:]
            lanes = lax.broadcasted_iota(jnp.int32, coeffs.shape, 1)
            coeffs = jnp.where(lanes < far_ranks[s], coeffs, 0.0)
            high, low = split(jnp.concatenate([coeffs, swap_rows(coeffs)], axis=1))
            for i in range(1, per_far):
                near(s * per_far + i)
            both = dot(jnp.concatenate([high, low], axis=0), right_far[0, s])
            terms[n_near + s, :width] = fold(both) + dot(high, right_far[1, s])

        for s in range(n_far * step // STEPS, n_far * (step + 1) // STEPS):
            body(s)

    def make_sums(k):
        width, rows = plan.width[k], plan.rows(k)
        for j in list(range(1, n_dir)) + [0]:
            for i in range(n_row):
                q = row_of(i)
                target = c * n_row + lax.rem(d + j, n_dir) * per_dir + q // n_dir
                lanes = pl.ds(pl.multiple_of(lax.rem(q, n_dir) * piece, piece), piece)
                gains = [
                    jnp.where((near_pairs[1, s] == target) & (s < counts[0, 0]), 1.0, 0.0) for s in range(n_near)
                ] + [jnp.where((far_pairs[1, s] == target) & (s < counts[0, 1]), 1.0, 0.0) for s in range(n_far)]
                total = terms[0, :width, lanes] * gains[0]
                for s in range(1, n_near + n_far):
                    total = total + terms[s, :width, lanes] * gains[s]
                parts[j, i, rows] = total
                if j > 0 and plan.row_wide[k] < width:
                    send_part(k, j, i).start()
                if i == n_cross and plan.row_wide[k] > 0:
                    send_sum(k, i, j).start()
                if i < n_cross and plan.row_wide[k] > 0:

                    @pl.when(jnp.logical_not(gathers(i)))
                    def _():
                        send_pair(k, i, j).start()

    def add_part(k, step):
        rows = plan.dir_rows(k)
        for i in range(n_row * step // STEPS, n_row * (step + 1) // STEPS):
            total = parts[0, i, rows]
            for j in range(1, n_dir):
                send_part(k, j, i).wait_recv()
                total = total + dir_parts[j - 1, i, rows]
            parts[0, i, rows] = total
            if i == n_cross:
                send_row(k, i, r // 2).start()
            if i < n_cross:

                @pl.when(jnp.logical_not(gathers(i)))
                def _():
                    pair_part(k, i).start()

    def add_far(k, step):
        rows = plan.dir_rows(k)
        for i in range(n_row * step // STEPS, min(n_cross, n_row * (step + 1) // STEPS)):

            @pl.when(gathers(i))
            def _():
                pair_part(k, i).wait_recv()
                parts[0, i, rows] = parts[0, i, rows] + pair_dir[i, rows]
                send_row(k, i, r // 2).start()

    def add_pairs(k):
        rows, slots = plan.row_rows(k), plan.row_slots(k)
        for i in range(n_cross):

            @pl.when(gathers(i))
            def _():
                remote(
                    parts.at[:, i, rows], pair_in.at[i, :, slots], q_send.at[0], a_recv.at[k, i], row_peer(n_cross)
                ).wait_recv()
                for j in list(range(1, n_dir)) + [0]:
                    parts[j, i, rows] = parts[j, i, rows] + pair_in[i, j, slots]
                    send_sum(k, i, j).start()

    def add_rows(k):
        rows, slots = plan.row_rows(k), plan.row_slots(k)
        for p in range(n_row // 2):
            remote(
                parts.at[:, own, rows], row_in.at[p, :, slots], q_send.at[0], q_recv.at[k, p], row_peer(n_cross)
            ).wait_recv()
        for j in list(range(1, n_dir)) + [0]:
            total = parts[j, own, rows]
            for p in range(n_row // 2):
                total = total + row_in[p, j, slots]
            parts[j, own, rows] = total
            if j > 0:
                send_last(k, j).start()

    def place(k, start, total):
        half, at = plan.half[k], plan.first[k]
        stop = start + total.shape[0]
        if start < half:
            cut = min(stop, half)
            totals[at + start : at + cut] = total[: cut - start]
        if stop > half:
            cut = max(start, half)
            base = wide // 2 + at - half
            totals[base + cut : base + stop] = total[cut - start :]

    def finish_dir(k):
        rows = plan.dir_rows(k)
        total = parts[0, own, rows]
        for p in range(n_row // 2):
            send_row(k, own, p).wait_recv()
            total = total + row_dir[p, rows]
        place(k, 0, total)

    def finish_row(k):
        rows, slots = plan.row_rows(k), plan.row_slots(k)
        total = parts[0, own, rows]
        for j in range(1, n_dir):
            send_last(k, j).wait_recv()
            total = total + last_in[j - 1, slots]
        place(k, plan.width[k] - plan.row_wide[k], total)

    def put(first, last):
        for base in (0, wide // 2):
            columns = slice(base + first, base + last)
            placed[:, columns] = totals[columns].T
            copy = pltpu.make_async_copy(placed.at[:, columns], out.at[:, columns], o_sem.at[len(put_copies)])
            copy.start()
            put_copies.append(copy)

    def drain():
        for j in range(1, n_dir):
            remote(sent, dir_in.at[j - 1], d_send.at[j - 1], d_recv.at[0, 0], dir_peer(1)).wait_send()
        for j in range(1, n_x):
            remote(gathered.at[0], gathered.at[0], x_send.at[j - 1], x_recv.at[0, 0], x_peer(1)).wait_send()
        all_of = gathered.at[pl.ds(0, n_x)]
        remote(all_of, all_of, c_send.at[0], c_recv.at[0, 0], (d, r, partner)).wait_send()
        dir_rows, row_rows = pl.ds(0, plan.dir_total), pl.ds(0, sum(plan.row_wide))
        if plan.dir_total > 0:
            all_of = parts.at[pl.ds(1, n_dir - 1), :, dir_rows]
            remote(all_of, all_of, p_send.at[0], p_recv.at[0, 0, 0], dir_peer(1)).wait_send()
            all_of = parts.at[0, pl.ds(0, own), dir_rows]
            remote(all_of, all_of, r_send.at[0], r_recv.at[0, 0], row_peer(n_cross)).wait_send()
        if sum(plan.row_wide) > 0:
            all_of = parts.at[:, pl.ds(0, own), row_rows]
            remote(all_of, all_of, q_send.at[0], q_recv.at[0, 0], row_peer(n_cross)).wait_send()
            all_of = parts.at[pl.ds(1, n_dir - 1), own, row_rows]
            remote(all_of, all_of, l_send.at[0], l_recv.at[0, 0], dir_peer(1)).wait_send()
        for copy in put_copies:
            copy.wait()

    put_copies = []

    for load in inputs:
        load.wait()
    for item in range(stages):
        load_item(item).start()
    for s in range(min(2, n_far)):
        for load in load_far(s):
            load.start()
    cot_t[...] = cot[...].T
    for k in range(chunks):
        right_sides(k)
        if k == 1:
            pl.semaphore_wait(barrier, len(peers))
        for i in ((0, 1) if k == 1 else (k,) if k > 1 else ()):
            for j in range(1, n_dir):
                send_dir(i, j).start()

    waiting = {k: (plan.row_wide[k] > 0) + (plan.row_wide[k] < plan.width[k]) for k in range(chunks)}
    put_at = [0]

    def finished(k):
        waiting[k] -= 1
        ends = [stop for stop in range(128, wide // 2 + 1, 128) if stop > put_at[0]]
        for stop in ends:
            if any(waiting[i] for i in range(chunks) if plan.first[i] < stop):
                return
            put(put_at[0], stop)
            put_at[0] = stop

    calls = {
        "convert": lambda i: convert(n_near * i // STEPS, n_near * (i + 1) // STEPS),
        "pack": pack_far,
        "dirs": add_dirs,
        "relay": relay,
        "sides": make_sides,
        "near": multiply,
        "sums": make_sums,
        "part": add_part,
        "far": add_far,
        "pairs": add_pairs,
        "rows": add_rows,
        "last": finish_dir,
        "end": finish_row,
    }
    for name, *at in ORDER:
        calls[name](*at)
        if name in ("last", "end"):
            finished(at[0])
    drain()


def shards(
    cotangent, radiation, near_z, near_pairs, far_ut, far_vt, far_pairs, far_ranks, block_counts
):
    n_dir, n_row, n_col = (lax.axis_size(name) for name in ("dir", "row", "col"))
    deep, wide = cotangent.shape
    small = n_row * n_col <= 16
    plan = Plan(wide, small)
    chunks, most = plan.chunks, max(plan.width)
    block = near_z.shape[2]
    n_near, n_far, rank_most = near_z.shape[1], far_ut.shape[1], far_ut.shape[2]
    n_x = n_col // CORES
    piece = block // n_dir
    stages = min(6 if small else 2, 2 * n_near)
    rank_pad = -(-rank_most // 128) * 128
    smem = pl.BlockSpec(memory_space=pltpu.SMEM)
    anywhere = pl.BlockSpec(memory_space=pl.ANY)
    dma = pltpu.SemaphoreType.DMA
    return pl.pallas_call(
        functools.partial(kernel, n_dir, n_row, n_col, plan),
        out_shape=jax.ShapeDtypeStruct((piece, wide), F32),
        in_specs=[smem] * 4 + [anywhere] * 5,
        out_specs=anywhere,
        scratch_shapes=[
            pltpu.VMEM((piece, wide), F32),
            pltpu.VMEM((deep, wide), BF16),
            pltpu.VMEM(radiation.shape, BF16),
            pltpu.VMEM((n_near, 2 * block, block), BF16),
            pltpu.VMEM((n_near, 2 * block, block), BF16),
            pltpu.VMEM((stages, block, block), F32),
            pltpu.VMEM((2, 4, rank_most, block), F32),
            pltpu.VMEM((n_far, 2 * block, 2 * rank_pad), BF16),
            pltpu.VMEM((2, n_far, 2 * rank_pad, block), BF16),
            pltpu.VMEM((wide, deep), BF16),
            pltpu.VMEM((wide, piece), F32),
            pltpu.VMEM((wide, block), F32),
            pltpu.VMEM((n_dir - 1, wide, block), F32),
            pltpu.VMEM((n_col, wide, block), F32),
            pltpu.VMEM((n_col, 2 * most, 2 * block), BF16),
            pltpu.VMEM((n_near + n_far, most, block), F32),
            pltpu.VMEM((n_dir, n_row, wide, piece), F32),
            pltpu.VMEM((n_dir - 1, n_row, wide, piece), F32),
            pltpu.VMEM((n_row - 2, wide, piece), F32),
            pltpu.VMEM((n_row // 2, wide, piece), F32),
            pltpu.VMEM((n_row - 2, n_dir, plan.row_total, piece), F32),
            pltpu.VMEM((n_row // 2, n_dir, plan.row_total, piece), F32),
            pltpu.VMEM((n_dir - 1, plan.row_total, piece), F32),
            dma((3,)),
            dma((stages,)),
            dma((2, 4)),
            dma((n_dir - 1,)),
            dma((chunks, n_dir - 1)),
            dma((n_x - 1,)),
            dma((chunks, n_x - 1)),
            dma((1,)),
            dma((chunks, n_x)),
            dma((1,)),
            dma((chunks, n_dir - 1, n_row)),
            dma((1,)),
            dma((chunks, n_row - 2)),
            dma((chunks, n_row // 2)),
            dma((1,)),
            dma((chunks, n_row - 2)),
            dma((chunks, n_row // 2)),
            dma((1,)),
            dma((chunks, n_dir - 1)),
            dma((4,)),
        ],
        compiler_params=pltpu.CompilerParams(
            collective_id=0, has_side_effects=True, vmem_limit_bytes=67043328
        ),
    )(near_pairs.T, far_pairs.T, far_ranks, block_counts, cotangent, radiation, near_z, far_ut, far_vt)


def solution(mesh):
    return jax.shard_map(
        shards,
        mesh=mesh,
        in_specs=(
            P("dir", None),
            P(None, ("row", "col"), "dir"),
            P(None, ("dir", "row", "col"), None, None),
            P(("dir", "row", "col"), None),
            P(None, ("dir", "row", "col"), None, None),
            P(None, ("dir", "row", "col"), None, None),
            P(("dir", "row", "col"), None),
            P(("dir", "row", "col")),
            P(("dir", "row", "col"), None),
        ),
        out_specs=P(("col", "dir", "row"), None),
        check_vma=False,
    )
```

```python
import functools

import jax
import jax.numpy as jnp
from jax import lax
from jax.experimental import pallas as pl
from jax.experimental.pallas import tpu as pltpu
from jax.sharding import PartitionSpec as P

CORES = 2
MESH = pl.DeviceIdType.MESH
F32 = jnp.float32
BF16 = jnp.bfloat16
NT = (((1,), (1,)), ((), ()))
PARTS = 8
SIZES = (1, 1, 2, 2, 2)
ROW_FIRST = (0.625, 0.75, 0.5, 0, 0)
STEPS = 4
ORDER = (
    ("convert", 0), ("convert", 1), ("convert", 2), ("dirs", 0), ("convert", 3), ("pack",), ("dirs", 1), ("relay", 0),
    ("sides", 0), ("near", 0, 0), ("near", 0, 1), ("relay", 1), ("near", 0, 2), ("dirs", 2), ("near", 0, 3),
    ("sums", 0), ("sides", 1), ("near", 1, 0), ("near", 1, 1), ("near", 1, 2), ("near", 1, 3), ("sums", 1),
    ("dirs", 3), ("pairs", 0), ("relay", 2), ("sides", 2), ("near", 2, 0), ("near", 2, 1), ("dirs", 4),
    ("near", 2, 2), ("relay", 3), ("rows", 0), ("part", 0, 0), ("part", 0, 1), ("part", 0, 2), ("pairs", 1),
    ("near", 2, 3), ("part", 0, 3), ("part", 1, 0), ("part", 1, 1), ("part", 1, 2), ("sums", 2), ("far", 0, 0),
    ("part", 1, 3), ("far", 0, 1), ("sides", 3), ("near", 3, 0), ("far", 1, 0), ("far", 1, 1), ("near", 3, 1),
    ("part", 2, 0), ("near", 3, 2), ("relay", 4), ("part", 2, 1), ("rows", 1), ("near", 3, 3), ("part", 2, 2),
    ("sums", 3), ("part", 2, 3), ("sides", 4), ("near", 4, 0), ("near", 4, 1), ("pairs", 2), ("near", 4, 2),
    ("part", 3, 0), ("near", 4, 3), ("far", 2, 0), ("sums", 4), ("far", 2, 1), ("part", 3, 1), ("end", 0),
    ("last", 0), ("last", 1), ("end", 1), ("part", 3, 2), ("rows", 2), ("far", 3, 0), ("part", 3, 3), ("last", 2),
    ("far", 3, 1), ("part", 4, 0), ("part", 4, 1), ("last", 3), ("far", 4, 0), ("part", 4, 2), ("far", 4, 1),
    ("part", 4, 3), ("end", 2), ("last", 4),
)


def dot(left, right):
    return jnp.dot(left, right, preferred_element_type=F32)


def dot_nt(left, right):
    return lax.dot_general(left, right, NT, preferred_element_type=F32)


def split(values):
    high = values.astype(BF16)
    return high, (values - high.astype(F32)).astype(BF16)


def swap_rows(values):
    half = values.shape[0] // 2
    return jnp.concatenate([-values[half:], values[:half]], axis=0)


def fold(values):
    half = values.shape[0] // 2
    return values[:half] + values[half:]


class Plan:
    def __init__(self, wide, small):
        unit = wide // 2 // PARTS
        self.half = [unit * size for size in SIZES]
        self.width = [2 * half for half in self.half]
        self.first = [sum(self.half[:k]) for k in range(len(self.half))]
        self.row_wide = [int(width * share) for width, share in zip(self.width, ROW_FIRST)]
        if not small:
            self.row_wide = [min(8, rows) for rows in self.row_wide]
        self.row_at = [sum(self.row_wide[:k]) for k in range(len(self.half))]
        self.row_total = max(8, sum(self.row_wide))
        self.dir_total = sum(self.width) - sum(self.row_wide)
        self.chunks = len(self.half)

    def rows(self, k):
        return slice(2 * self.first[k], 2 * self.first[k] + self.width[k])

    def dir_rows(self, k):
        start = 2 * self.first[k]
        return slice(start, start + self.width[k] - self.row_wide[k])

    def row_rows(self, k):
        stop = 2 * self.first[k] + self.width[k]
        return slice(stop - self.row_wide[k], stop)

    def row_slots(self, k):
        return slice(self.row_at[k], self.row_at[k] + self.row_wide[k])


def kernel(
    n_dir, n_row, n_col, plan,
    near_pairs, far_pairs, far_ranks, counts, cot_hbm, rad_hbm, near_z, far_ut, far_vt,
    out,
    cot, rad, z_high, z_low, stage, far_stage, left_far, right_far, cot_t, totals, sent, dir_in, gathered, sides, terms,
    parts, dir_parts, pair_dir, row_dir, pair_in, row_in, last_in,
    in_sem, stage_sem, far_sem, d_send, d_recv, x_send, x_recv, c_send, c_recv, p_send, p_recv, r_send, f_recv, r_recv,
    q_send, a_recv, q_recv, l_send, l_recv,
):
    chunks = plan.chunks
    wide = cot.shape[1]
    stages = stage.shape[0]
    rank_most, rank_pad = far_ut.shape[2], left_far.shape[2] // 2
    n_near, n_far = near_z.shape[1], far_ut.shape[1]
    block = near_z.shape[2]
    piece = block // n_dir
    n_x = n_col // CORES
    per_dir = n_row // n_dir
    n_cross, own = n_row - 2, n_row - 1
    d = lax.axis_index("dir")
    r = lax.axis_index("row")
    c = lax.axis_index("col")
    x, core = c // CORES, c % CORES
    partner = x * CORES + (CORES - 1 - core)
    row_pair = r + 1 - 2 * lax.rem(r, 2)

    def dir_peer(j):
        return (lax.rem(d + j, n_dir), r, c)

    def x_peer(j):
        return (d, r, lax.rem(x + j, n_x) * CORES + core)

    def row_of(i):
        base = 2 * (r // 2)
        if i < n_cross:
            return jnp.where(r < n_row // 2, lax.rem(base + n_row - 1 - i, n_row), lax.rem(base + 2 + i, n_row))
        return row_pair if i == n_cross else r

    def row_peer(i):
        return (d, row_of(i), c)

    def gathers(i):
        return (row_of(i) > r) == (lax.rem(r, 2) == 1)

    def from_x(j, core_of):
        return lax.rem(x + n_x - j, n_x) * CORES + core_of

    def remote(src, dst, send, recv, device):
        return pltpu.make_async_remote_copy(
            src_ref=src, dst_ref=dst, send_sem=send, recv_sem=recv, device_id=device, device_id_type=MESH
        )

    peers = [dir_peer(j) for j in range(1, n_dir)]
    peers += [x_peer(j) for j in range(1, n_x)]
    peers += [row_peer(i) for i in range(own)]
    peers.append((d, r, partner))
    barrier = pltpu.get_barrier_semaphore()
    for device in peers:
        pl.semaphore_signal(barrier, inc=1, device_id=device, device_id_type=MESH)

    inputs = [pltpu.make_async_copy(cot_hbm, cot, in_sem.at[0])]
    inputs += [pltpu.make_async_copy(rad_hbm.at[part], rad.at[part], in_sem.at[1 + part]) for part in range(2)]
    for load in inputs:
        load.start()

    def load_item(item):
        slot, part = item // 2, lax.rem(item, 2)
        return pltpu.make_async_copy(
            near_z.at[part, slot], stage.at[lax.rem(item, stages)], stage_sem.at[lax.rem(item, stages)]
        )

    def load_far(s):
        side = lax.rem(s, 2)
        return [
            pltpu.make_async_copy(source.at[part, s], far_stage.at[side, 2 * i + part], far_sem.at[side, 2 * i + part])
            for i, source in enumerate((far_ut, far_vt))
            for part in range(2)
        ]

    def send_dir(k, j):
        rows = plan.rows(k)
        return remote(sent.at[rows], dir_in.at[j - 1, rows], d_send.at[j - 1], d_recv.at[k, j - 1], dir_peer(j))

    def send_x(k, j, which=None):
        block_of = gathered.at[c if which is None else which, plan.rows(k)]
        return remote(block_of, block_of, x_send.at[j - 1], x_recv.at[k, j - 1], x_peer(j))

    def send_core(k, j, core_of):
        block_of = gathered.at[from_x(j, core_of), plan.rows(k)]
        return remote(block_of, block_of, c_send.at[0], c_recv.at[k, j], (d, r, partner))

    def send_part(k, j, i):
        rows = plan.dir_rows(k)
        return remote(
            parts.at[j, i, rows], dir_parts.at[j - 1, i, rows], p_send.at[0], p_recv.at[k, j - 1, i], dir_peer(j)
        )

    def pair_part(k, i):
        rows = plan.dir_rows(k)
        return remote(parts.at[0, i, rows], pair_dir.at[i, rows], r_send.at[0], f_recv.at[k, i], row_peer(n_cross))

    def send_row(k, i, p):
        rows = plan.dir_rows(k)
        return remote(parts.at[0, i, rows], row_dir.at[p, rows], r_send.at[0], r_recv.at[k, p], row_peer(i))

    def send_pair(k, i, j):
        return remote(
            parts.at[j, i, plan.row_rows(k)],
            pair_in.at[i, j, plan.row_slots(k)],
            q_send.at[0],
            a_recv.at[k, i],
            row_peer(n_cross),
        )

    def send_sum(k, i, j):
        return remote(
            parts.at[j, i, plan.row_rows(k)],
            row_in.at[r // 2, j, plan.row_slots(k)],
            q_send.at[0],
            q_recv.at[k, r // 2],
            row_peer(i),
        )

    def send_last(k, j):
        return remote(
            parts.at[j, own, plan.row_rows(k)],
            last_in.at[j - 1, plan.row_slots(k)],
            l_send.at[0],
            l_recv.at[k, j - 1],
            dir_peer(j),
        )

    def right_sides(first, last):
        at, stop = plan.first[first], plan.first[last] + plan.half[last]
        half = stop - at
        left = jnp.concatenate([cot_t[at:stop], cot_t[wide // 2 + at : wide // 2 + stop]], axis=0)
        result = dot_nt(left, rad[0]) + dot_nt(swap_rows(left), rad[1])
        for k in range(first, last + 1):
            base, size = plan.first[k] - at, plan.half[k]
            rows = plan.rows(k)
            sent[rows.start : rows.start + size] = result[base : base + size]
            sent[rows.start + size : rows.stop] = result[half + base : half + base + size]

    def convert(first, last):
        def body(item, carry):
            load_item(item).wait()
            high, low = split(stage[lax.rem(item, stages)])
            rows = pl.ds(pl.multiple_of(lax.rem(item, 2) * block, block), block)
            z_high[item // 2, rows, :] = high
            z_low[item // 2, rows, :] = low

            @pl.when(item + stages < 2 * n_near)
            def _():
                load_item(item + stages).start()

            return carry

        lax.fori_loop(2 * first, 2 * last, body, 0)

    def pack_far():
        rest = jnp.zeros((rank_pad - rank_most, block), F32)

        def body(s, carry):
            for load in load_far(s):
                load.wait()
            side = lax.rem(s, 2)
            for part in range(2):
                factor = jnp.concatenate([far_stage[side, part], rest], axis=0)
                high, low = split(factor.T)
                rows = slice(part * block, (part + 1) * block)
                left_far[s, rows, :rank_pad] = high
                left_far[s, rows, rank_pad:] = low
                factor = jnp.concatenate([far_stage[side, 2 + part], rest], axis=0)
                high, low = split(factor)
                rows = slice(part * rank_pad, (part + 1) * rank_pad)
                right_far[0, s, rows, :] = high
                right_far[1, s, rows, :] = low

            @pl.when(s + 2 < n_far)
            def _():
                for load in load_far(s + 2):
                    load.start()

            return carry

        lax.fori_loop(0, n_far, body, 0)

    def add_dirs(k):
        rows = plan.rows(k)
        for j in range(1, n_dir):
            send_dir(k, j).wait_recv()
        total = sent[rows]
        for j in range(1, n_dir):
            total = total + dir_in[j - 1, rows]
        gathered[c, rows] = total
        for j in range(1, n_x):
            send_x(k, j).start()
        send_core(k, 0, core).start()

    def relay(k):
        for j in range(1, n_x):
            send_x(k, j, from_x(j, core)).wait_recv()
            send_core(k, j, core).start()

    per_far = n_near // n_far

    def make_sides(k):
        width, rows = plan.width[k], plan.rows(k)
        for j in range(n_x):
            send_core(k, j, CORES - 1 - core).wait_recv()

        def side(q, carry):
            values = gathered[q, rows]
            high, low = split(jnp.concatenate([values, swap_rows(values)], axis=1))
            sides[q, :width] = high
            sides[q, width : 2 * width] = low
            return carry

        lax.fori_loop(0, n_col, side, 0)

    def multiply(k, step):
        width = plan.width[k]

        def near(s):
            left = sides[lax.rem(near_pairs[0, s], n_col), : 2 * width]
            terms[s, :width] = fold(dot(left, z_high[s])) + dot(left[:width], z_low[s])

        def body(s):
            both = dot(sides[lax.rem(far_pairs[0, s], n_col), : 2 * width], left_far[s])
            near(s * per_far)
            coeffs = fold(both[:, :rank_pad]) + both[:width, rank_pad:]
            lanes = lax.broadcasted_iota(jnp.int32, coeffs.shape, 1)
            coeffs = jnp.where(lanes < far_ranks[s], coeffs, 0.0)
            high, low = split(jnp.concatenate([coeffs, swap_rows(coeffs)], axis=1))
            for i in range(1, per_far):
                near(s * per_far + i)
            both = dot(jnp.concatenate([high, low], axis=0), right_far[0, s])
            terms[n_near + s, :width] = fold(both) + dot(high, right_far[1, s])

        for s in range(n_far * step // STEPS, n_far * (step + 1) // STEPS):
            body(s)

    def make_sums(k):
        width, rows = plan.width[k], plan.rows(k)
        for j in list(range(1, n_dir)) + [0]:
            for i in range(n_row):
                q = row_of(i)
                target = c * n_row + lax.rem(d + j, n_dir) * per_dir + q // n_dir
                lanes = pl.ds(pl.multiple_of(lax.rem(q, n_dir) * piece, piece), piece)
                gains = [
                    jnp.where((near_pairs[1, s] == target) & (s < counts[0, 0]), 1.0, 0.0) for s in range(n_near)
                ] + [jnp.where((far_pairs[1, s] == target) & (s < counts[0, 1]), 1.0, 0.0) for s in range(n_far)]
                total = terms[0, :width, lanes] * gains[0]
                for s in range(1, n_near + n_far):
                    total = total + terms[s, :width, lanes] * gains[s]
                parts[j, i, rows] = total
                if j > 0 and plan.row_wide[k] < width:
                    send_part(k, j, i).start()
                if i == n_cross and plan.row_wide[k] > 0:
                    send_sum(k, i, j).start()
                if i < n_cross and plan.row_wide[k] > 0:

                    @pl.when(jnp.logical_not(gathers(i)))
                    def _():
                        send_pair(k, i, j).start()

    def add_part(k, step):
        rows = plan.dir_rows(k)
        for i in range(n_row * step // STEPS, n_row * (step + 1) // STEPS):
            total = parts[0, i, rows]
            for j in range(1, n_dir):
                send_part(k, j, i).wait_recv()
                total = total + dir_parts[j - 1, i, rows]
            parts[0, i, rows] = total
            if i == n_cross:
                send_row(k, i, r // 2).start()
            if i < n_cross:

                @pl.when(jnp.logical_not(gathers(i)))
                def _():
                    pair_part(k, i).start()

    def add_far(k, step):
        rows = plan.dir_rows(k)
        for i in range(n_row * step // STEPS, min(n_cross, n_row * (step + 1) // STEPS)):

            @pl.when(gathers(i))
            def _():
                pair_part(k, i).wait_recv()
                parts[0, i, rows] = parts[0, i, rows] + pair_dir[i, rows]
                send_row(k, i, r // 2).start()

    def add_pairs(k):
        rows, slots = plan.row_rows(k), plan.row_slots(k)
        for i in range(n_cross):

            @pl.when(gathers(i))
            def _():
                remote(
                    parts.at[:, i, rows], pair_in.at[i, :, slots], q_send.at[0], a_recv.at[k, i], row_peer(n_cross)
                ).wait_recv()
                for j in list(range(1, n_dir)) + [0]:
                    parts[j, i, rows] = parts[j, i, rows] + pair_in[i, j, slots]
                    send_sum(k, i, j).start()

    def add_rows(k):
        rows, slots = plan.row_rows(k), plan.row_slots(k)
        for p in range(n_row // 2):
            remote(
                parts.at[:, own, rows], row_in.at[p, :, slots], q_send.at[0], q_recv.at[k, p], row_peer(n_cross)
            ).wait_recv()
        for j in list(range(1, n_dir)) + [0]:
            total = parts[j, own, rows]
            for p in range(n_row // 2):
                total = total + row_in[p, j, slots]
            parts[j, own, rows] = total
            if j > 0:
                send_last(k, j).start()

    def place(k, start, total):
        half, at = plan.half[k], plan.first[k]
        stop = start + total.shape[0]
        if start < half:
            cut = min(stop, half)
            totals[at + start : at + cut] = total[: cut - start]
        if stop > half:
            cut = max(start, half)
            base = wide // 2 + at - half
            totals[base + cut : base + stop] = total[cut - start :]

    def finish_dir(k):
        rows = plan.dir_rows(k)
        total = parts[0, own, rows]
        for p in range(n_row // 2):
            send_row(k, own, p).wait_recv()
            total = total + row_dir[p, rows]
        place(k, 0, total)

    def finish_row(k):
        rows, slots = plan.row_rows(k), plan.row_slots(k)
        total = parts[0, own, rows]
        for j in range(1, n_dir):
            send_last(k, j).wait_recv()
            total = total + last_in[j - 1, slots]
        place(k, plan.width[k] - plan.row_wide[k], total)

    def put(first, last):
        for base in (0, wide // 2):
            columns = slice(base + first, base + last)
            out[:, columns] = totals[columns].T

    def drain():
        for j in range(1, n_dir):
            remote(sent, dir_in.at[j - 1], d_send.at[j - 1], d_recv.at[0, 0], dir_peer(1)).wait_send()
        for j in range(1, n_x):
            remote(gathered.at[0], gathered.at[0], x_send.at[j - 1], x_recv.at[0, 0], x_peer(1)).wait_send()
        all_of = gathered.at[pl.ds(0, n_x)]
        remote(all_of, all_of, c_send.at[0], c_recv.at[0, 0], (d, r, partner)).wait_send()
        dir_rows, row_rows = pl.ds(0, plan.dir_total), pl.ds(0, sum(plan.row_wide))
        if plan.dir_total > 0:
            all_of = parts.at[pl.ds(1, n_dir - 1), :, dir_rows]
            remote(all_of, all_of, p_send.at[0], p_recv.at[0, 0, 0], dir_peer(1)).wait_send()
            all_of = parts.at[0, pl.ds(0, own), dir_rows]
            remote(all_of, all_of, r_send.at[0], r_recv.at[0, 0], row_peer(n_cross)).wait_send()
        if sum(plan.row_wide) > 0:
            all_of = parts.at[:, pl.ds(0, own), row_rows]
            remote(all_of, all_of, q_send.at[0], q_recv.at[0, 0], row_peer(n_cross)).wait_send()
            all_of = parts.at[pl.ds(1, n_dir - 1), own, row_rows]
            remote(all_of, all_of, l_send.at[0], l_recv.at[0, 0], dir_peer(1)).wait_send()

    inputs[0].wait()
    cot_t[...] = cot[...].T
    for load in inputs[1:]:
        load.wait()
    for item in range(stages):
        load_item(item).start()
    for s in range(min(2, n_far)):
        for load in load_far(s):
            load.start()
    early = next(k for k in range(chunks) if plan.first[k] + plan.half[k] >= 2 * wide // (2 * PARTS))
    for group in ((0, early), (early + 1, chunks - 1)):
        right_sides(*group)
        if group[0] == 0:
            pl.semaphore_wait(barrier, len(peers))
        for k in range(group[0], group[1] + 1):
            for j in range(1, n_dir):
                send_dir(k, j).start()

    waiting = {k: (plan.row_wide[k] > 0) + (plan.row_wide[k] < plan.width[k]) for k in range(chunks)}
    put_at = [0]

    def finished(k):
        waiting[k] -= 1
        ends = [stop for stop in range(128, wide // 2 + 1, 128) if stop > put_at[0]]
        for stop in ends:
            if any(waiting[i] for i in range(chunks) if plan.first[i] < stop):
                return
            put(put_at[0], stop)
            put_at[0] = stop

    calls = {
        "convert": lambda i: convert(n_near * i // STEPS, n_near * (i + 1) // STEPS),
        "pack": pack_far,
        "dirs": add_dirs,
        "relay": relay,
        "sides": make_sides,
        "near": multiply,
        "sums": make_sums,
        "part": add_part,
        "far": add_far,
        "pairs": add_pairs,
        "rows": add_rows,
        "last": finish_dir,
        "end": finish_row,
    }
    for name, *at in ORDER:
        calls[name](*at)
        if name in ("last", "end"):
            finished(at[0])
    drain()


def shards(
    cotangent, radiation, near_z, near_pairs, far_ut, far_vt, far_pairs, far_ranks, block_counts
):
    n_dir, n_row, n_col = (lax.axis_size(name) for name in ("dir", "row", "col"))
    deep, wide = cotangent.shape
    small = n_row * n_col <= 16
    plan = Plan(wide, small)
    chunks, most = plan.chunks, max(plan.width)
    block = near_z.shape[2]
    n_near, n_far, rank_most = near_z.shape[1], far_ut.shape[1], far_ut.shape[2]
    n_x = n_col // CORES
    piece = block // n_dir
    stages = min(6 if small else 2, 2 * n_near)
    rank_pad = -(-rank_most // 128) * 128
    smem = pl.BlockSpec(memory_space=pltpu.SMEM)
    anywhere = pl.BlockSpec(memory_space=pl.ANY)
    dma = pltpu.SemaphoreType.DMA
    return pl.pallas_call(
        functools.partial(kernel, n_dir, n_row, n_col, plan),
        out_shape=pltpu.VMEM((piece, wide), F32),
        in_specs=[smem] * 4 + [anywhere] * 5,
        out_specs=pl.BlockSpec(memory_space=pltpu.VMEM),
        scratch_shapes=[
            pltpu.VMEM((deep, wide), BF16),
            pltpu.VMEM(radiation.shape, BF16),
            pltpu.VMEM((n_near, 2 * block, block), BF16),
            pltpu.VMEM((n_near, 2 * block, block), BF16),
            pltpu.VMEM((stages, block, block), F32),
            pltpu.VMEM((2, 4, rank_most, block), F32),
            pltpu.VMEM((n_far, 2 * block, 2 * rank_pad), BF16),
            pltpu.VMEM((2, n_far, 2 * rank_pad, block), BF16),
            pltpu.VMEM((wide, deep), BF16),
            pltpu.VMEM((wide, piece), F32),
            pltpu.VMEM((wide, block), F32),
            pltpu.VMEM((n_dir - 1, wide, block), F32),
            pltpu.VMEM((n_col, wide, block), F32),
            pltpu.VMEM((n_col, 2 * most, 2 * block), BF16),
            pltpu.VMEM((n_near + n_far, most, block), F32),
            pltpu.VMEM((n_dir, n_row, wide, piece), F32),
            pltpu.VMEM((n_dir - 1, n_row, wide, piece), F32),
            pltpu.VMEM((n_row - 2, wide, piece), F32),
            pltpu.VMEM((n_row // 2, wide, piece), F32),
            pltpu.VMEM((n_row - 2, n_dir, plan.row_total, piece), F32),
            pltpu.VMEM((n_row // 2, n_dir, plan.row_total, piece), F32),
            pltpu.VMEM((n_dir - 1, plan.row_total, piece), F32),
            dma((3,)),
            dma((stages,)),
            dma((2, 4)),
            dma((n_dir - 1,)),
            dma((chunks, n_dir - 1)),
            dma((n_x - 1,)),
            dma((chunks, n_x - 1)),
            dma((1,)),
            dma((chunks, n_x)),
            dma((1,)),
            dma((chunks, n_dir - 1, n_row)),
            dma((1,)),
            dma((chunks, n_row - 2)),
            dma((chunks, n_row // 2)),
            dma((1,)),
            dma((chunks, n_row - 2)),
            dma((chunks, n_row // 2)),
            dma((1,)),
            dma((chunks, n_dir - 1)),
        ],
        compiler_params=pltpu.CompilerParams(
            collective_id=0, has_side_effects=True, vmem_limit_bytes=67043328 - 4 * piece * wide
        ),
    )(near_pairs.T, far_pairs.T, far_ranks, block_counts, cotangent, radiation, near_z, far_ut, far_vt)


def solution(mesh):
    return jax.shard_map(
        shards,
        mesh=mesh,
        in_specs=(
            P("dir", None),
            P(None, ("row", "col"), "dir"),
            P(None, ("dir", "row", "col"), None, None),
            P(("dir", "row", "col"), None),
            P(None, ("dir", "row", "col"), None, None),
            P(None, ("dir", "row", "col"), None, None),
            P(("dir", "row", "col"), None),
            P(("dir", "row", "col")),
            P(("dir", "row", "col"), None),
        ),
        out_specs=P(("col", "dir", "row"), None),
        check_vma=False,
    )
```

```python
import functools

import jax
import jax.numpy as jnp
from jax import lax
from jax.experimental import pallas as pl
from jax.experimental.pallas import tpu as pltpu
from jax.sharding import PartitionSpec as P

CORES = 2
MESH = pl.DeviceIdType.MESH
F32 = jnp.float32
BF16 = jnp.bfloat16
NT = (((1,), (1,)), ((), ()))
PARTS = 8
SIZES = (1, 1.5, 1.5, 2, 2)
ROW_FIRST = (0.875, 0.75, 0.25, 0, 0)
UNITS = (2, 2, 2, 2, 2)
STEPS = 4
ORDER = (
    ("convert", 0), ("convert", 1), ("dirs", 0), ("convert", 2), ("dirs", 1), ("convert", 3), ("pack",), ("dirs", 2),
    ("relay", 0), ("relay", 1), ("dirs", 3), ("sides", 0), ("near", 0, 0), ("near", 0, 1), ("dirs", 4), ("relay", 2),
    ("near", 0, 2), ("near", 0, 3), ("dirs", 5), ("relay", 3), ("sums", 0), ("sides", 1), ("near", 1, 0), ("dirs", 6),
    ("relay", 4), ("near", 1, 1), ("near", 1, 2), ("relay", 5), ("near", 1, 3), ("dirs", 7), ("sums", 1),
    ("sides", 2), ("relay", 6), ("near", 2, 0), ("dirs", 8), ("pairs", 0), ("near", 2, 1), ("near", 2, 2),
    ("relay", 7), ("near", 2, 3), ("dirs", 9), ("part", 0, 0), ("part", 0, 1), ("part", 0, 2), ("part", 0, 3),
    ("sums", 2), ("part", 1, 0), ("sides", 3), ("part", 1, 1), ("near", 3, 0), ("relay", 8), ("part", 1, 2),
    ("part", 1, 3), ("near", 3, 1), ("rows", 0), ("near", 3, 2), ("relay", 9), ("part", 2, 0), ("near", 3, 3),
    ("pairs", 1), ("part", 2, 1), ("sums", 3), ("far", 0, 0), ("part", 2, 2), ("far", 0, 1), ("sides", 4),
    ("near", 4, 0), ("part", 2, 3), ("near", 4, 1), ("pairs", 2), ("near", 4, 2), ("far", 1, 0), ("far", 1, 1),
    ("near", 4, 3), ("part", 3, 0), ("sums", 4), ("far", 2, 0), ("end", 0), ("rows", 1), ("last", 0), ("far", 2, 1),
    ("part", 3, 1), ("rows", 2), ("last", 1), ("part", 3, 2), ("far", 3, 0), ("last", 2), ("part", 3, 3),
    ("far", 3, 1), ("part", 4, 0), ("last", 3), ("part", 4, 1), ("far", 4, 0), ("part", 4, 2), ("far", 4, 1),
    ("part", 4, 3), ("end", 1), ("end", 2), ("last", 4),
)


def dot(left, right):
    return jnp.dot(left, right, preferred_element_type=F32)


def dot_nt(left, right):
    return lax.dot_general(left, right, NT, preferred_element_type=F32)


def split(values):
    high = values.astype(BF16)
    return high, (values - high.astype(F32)).astype(BF16)


def swap_rows(values):
    half = values.shape[0] // 2
    return jnp.concatenate([-values[half:], values[:half]], axis=0)


def fold(values):
    half = values.shape[0] // 2
    return values[:half] + values[half:]


class Plan:
    def __init__(self, wide, small):
        unit = wide // 2 // PARTS
        self.half = [int(unit * size) for size in SIZES]
        self.width = [2 * half for half in self.half]
        self.first = [sum(self.half[:k]) for k in range(len(self.half))]
        self.row_wide = [int(width * share) for width, share in zip(self.width, ROW_FIRST)]
        if not small:
            self.row_wide = [min(8, rows) for rows in self.row_wide]
        self.row_at = [sum(self.row_wide[:k]) for k in range(len(self.half))]
        self.row_total = max(8, sum(self.row_wide))
        self.dir_total = sum(self.width) - sum(self.row_wide)
        self.chunks = len(self.half)

    def units_of(self, k):
        return range(sum(UNITS[:k]), sum(UNITS[: k + 1]))

    def unit_rows(self, u):
        k = next(k for k in range(self.chunks) if u in self.units_of(k))
        size = self.width[k] // UNITS[k]
        start = 2 * self.first[k] + (u - sum(UNITS[:k])) * size
        return slice(start, start + size)

    def rows(self, k):
        return slice(2 * self.first[k], 2 * self.first[k] + self.width[k])

    def dir_rows(self, k):
        start = 2 * self.first[k]
        return slice(start, start + self.width[k] - self.row_wide[k])

    def row_rows(self, k):
        stop = 2 * self.first[k] + self.width[k]
        return slice(stop - self.row_wide[k], stop)

    def row_slots(self, k):
        return slice(self.row_at[k], self.row_at[k] + self.row_wide[k])


def kernel(
    n_dir, n_row, n_col, plan,
    near_pairs, far_pairs, far_ranks, counts, cot_hbm, rad_hbm, near_z, far_ut, far_vt,
    out,
    cot, rad, z_high, z_low, stage, far_stage, left_far, right_far, cot_t, totals, sent, dir_in, gathered, sides, terms,
    parts, dir_parts, pair_dir, row_dir, pair_in, row_in, last_in,
    in_sem, stage_sem, far_sem, d_send, d_recv, x_send, x_recv, c_send, c_recv, p_send, p_recv, r_send, f_recv, r_recv,
    q_send, a_recv, q_recv, l_send, l_recv,
):
    chunks = plan.chunks
    wide = cot.shape[1]
    stages = stage.shape[0]
    rank_most, rank_pad = far_ut.shape[2], left_far.shape[2] // 2
    n_near, n_far = near_z.shape[1], far_ut.shape[1]
    block = near_z.shape[2]
    piece = block // n_dir
    n_x = n_col // CORES
    per_dir = n_row // n_dir
    n_cross, own = n_row - 2, n_row - 1
    d = lax.axis_index("dir")
    r = lax.axis_index("row")
    c = lax.axis_index("col")
    x, core = c // CORES, c % CORES
    partner = x * CORES + (CORES - 1 - core)
    row_pair = r + 1 - 2 * lax.rem(r, 2)

    def dir_peer(j):
        return (lax.rem(d + j, n_dir), r, c)

    def x_peer(j):
        return (d, r, lax.rem(x + j, n_x) * CORES + core)

    def row_of(i):
        base = 2 * (r // 2)
        if i < n_cross:
            return jnp.where(r < n_row // 2, lax.rem(base + n_row - 1 - i, n_row), lax.rem(base + 2 + i, n_row))
        return row_pair if i == n_cross else r

    def row_peer(i):
        return (d, row_of(i), c)

    def gathers(i):
        return (row_of(i) > r) == (lax.rem(r, 2) == 1)

    def from_x(j, core_of):
        return lax.rem(x + n_x - j, n_x) * CORES + core_of

    def remote(src, dst, send, recv, device):
        return pltpu.make_async_remote_copy(
            src_ref=src, dst_ref=dst, send_sem=send, recv_sem=recv, device_id=device, device_id_type=MESH
        )

    peers = [dir_peer(j) for j in range(1, n_dir)]
    peers += [x_peer(j) for j in range(1, n_x)]
    peers += [row_peer(i) for i in range(own)]
    peers.append((d, r, partner))
    barrier = pltpu.get_barrier_semaphore()
    for device in peers:
        pl.semaphore_signal(barrier, inc=1, device_id=device, device_id_type=MESH)

    inputs = [pltpu.make_async_copy(cot_hbm, cot, in_sem.at[0])]
    inputs += [pltpu.make_async_copy(rad_hbm.at[part], rad.at[part], in_sem.at[1 + part]) for part in range(2)]
    for load in inputs:
        load.start()

    def load_item(item):
        slot, part = item // 2, lax.rem(item, 2)
        return pltpu.make_async_copy(
            near_z.at[part, slot], stage.at[lax.rem(item, stages)], stage_sem.at[lax.rem(item, stages)]
        )

    def load_far(s):
        side = lax.rem(s, 2)
        return [
            pltpu.make_async_copy(source.at[part, s], far_stage.at[side, 2 * i + part], far_sem.at[side, 2 * i + part])
            for i, source in enumerate((far_ut, far_vt))
            for part in range(2)
        ]

    def send_dir(u, j):
        rows = plan.unit_rows(u)
        return remote(sent.at[rows], dir_in.at[j - 1, rows], d_send.at[j - 1], d_recv.at[u, j - 1], dir_peer(j))

    def send_x(u, j, which=None):
        block_of = gathered.at[c if which is None else which, plan.unit_rows(u)]
        return remote(block_of, block_of, x_send.at[j - 1], x_recv.at[u, j - 1], x_peer(j))

    def send_core(u, j):
        k = next(k for k in range(chunks) if u in plan.units_of(k))
        block_of = gathered.at[from_x(j, core), plan.unit_rows(u)]
        return remote(block_of, block_of, c_send.at[0], c_recv.at[k], (d, r, partner))

    def send_part(k, j, i):
        rows = plan.dir_rows(k)
        return remote(
            parts.at[j, i, rows], dir_parts.at[j - 1, i, rows], p_send.at[0], p_recv.at[k, j - 1, i], dir_peer(j)
        )

    def pair_part(k, i):
        rows = plan.dir_rows(k)
        return remote(parts.at[0, i, rows], pair_dir.at[i, rows], r_send.at[0], f_recv.at[k, i], row_peer(n_cross))

    def send_row(k, i, p):
        rows = plan.dir_rows(k)
        return remote(parts.at[0, i, rows], row_dir.at[p, rows], r_send.at[0], r_recv.at[k], row_peer(i))

    def send_pair(k, i, j):
        return remote(
            parts.at[j, i, plan.row_rows(k)],
            pair_in.at[i, j, plan.row_slots(k)],
            q_send.at[0],
            a_recv.at[k, i],
            row_peer(n_cross),
        )

    def send_sum(k, i, j):
        return remote(
            parts.at[j, i, plan.row_rows(k)],
            row_in.at[r // 2, j, plan.row_slots(k)],
            q_send.at[0],
            q_recv.at[k],
            row_peer(i),
        )

    def send_last(k, j):
        return remote(
            parts.at[j, own, plan.row_rows(k)],
            last_in.at[j - 1, plan.row_slots(k)],
            l_send.at[0],
            l_recv.at[k, j - 1],
            dir_peer(j),
        )

    def right_sides(first, last):
        at, stop = plan.first[first], plan.first[last] + plan.half[last]
        half = stop - at
        left = jnp.concatenate([cot_t[at:stop], cot_t[wide // 2 + at : wide // 2 + stop]], axis=0)
        result = dot_nt(left, rad[0]) + dot_nt(swap_rows(left), rad[1])
        for k in range(first, last + 1):
            base, size = plan.first[k] - at, plan.half[k]
            rows = plan.rows(k)
            sent[rows.start : rows.start + size] = result[base : base + size]
            sent[rows.start + size : rows.stop] = result[half + base : half + base + size]

    def convert(first, last):
        def body(item, carry):
            load_item(item).wait()
            high, low = split(stage[lax.rem(item, stages)])
            rows = pl.ds(pl.multiple_of(lax.rem(item, 2) * block, block), block)
            z_high[item // 2, rows, :] = high
            z_low[item // 2, rows, :] = low

            @pl.when(item + stages < 2 * n_near)
            def _():
                load_item(item + stages).start()

            return carry

        lax.fori_loop(2 * first, 2 * last, body, 0)

    def pack_far():
        rest = jnp.zeros((rank_pad - rank_most, block), F32)

        def body(s, carry):
            for load in load_far(s):
                load.wait()
            side = lax.rem(s, 2)
            for part in range(2):
                factor = jnp.concatenate([far_stage[side, part], rest], axis=0)
                high, low = split(factor.T)
                rows = slice(part * block, (part + 1) * block)
                left_far[s, rows, :rank_pad] = high
                left_far[s, rows, rank_pad:] = low
                factor = jnp.concatenate([far_stage[side, 2 + part], rest], axis=0)
                high, low = split(factor)
                rows = slice(part * rank_pad, (part + 1) * rank_pad)
                right_far[0, s, rows, :] = high
                right_far[1, s, rows, :] = low

            @pl.when(s + 2 < n_far)
            def _():
                for load in load_far(s + 2):
                    load.start()

            return carry

        lax.fori_loop(0, n_far, body, 0)

    def add_dirs(u):
        rows = plan.unit_rows(u)
        for j in range(1, n_dir):
            send_dir(u, j).wait_recv()
        total = sent[rows]
        for j in range(1, n_dir):
            total = total + dir_in[j - 1, rows]
        gathered[c, rows] = total
        for j in range(1, n_x):
            send_x(u, j).start()
        send_core(u, 0).start()

    def relay(u):
        for j in range(1, n_x):
            send_x(u, j, from_x(j, core)).wait_recv()
            send_core(u, j).start()

    per_far = n_near // n_far

    def make_sides(k):
        width, rows = plan.width[k], plan.rows(k)
        all_of = gathered.at[pl.ds(0, n_x), rows]
        remote(all_of, all_of, c_send.at[0], c_recv.at[k], (d, r, partner)).wait_recv()

        def side(q, carry):
            values = gathered[q, rows]
            high, low = split(jnp.concatenate([values, swap_rows(values)], axis=1))
            sides[q, :width] = high
            sides[q, width : 2 * width] = low
            return carry

        lax.fori_loop(0, n_col, side, 0)

    def multiply(k, step):
        width = plan.width[k]

        def near(s):
            left = sides[lax.rem(near_pairs[0, s], n_col), : 2 * width]
            terms[s, :width] = fold(dot(left, z_high[s])) + dot(left[:width], z_low[s])

        def body(s):
            both = dot(sides[lax.rem(far_pairs[0, s], n_col), : 2 * width], left_far[s])
            near(s * per_far)
            coeffs = fold(both[:, :rank_pad]) + both[:width, rank_pad:]
            lanes = lax.broadcasted_iota(jnp.int32, coeffs.shape, 1)
            coeffs = jnp.where(lanes < far_ranks[s], coeffs, 0.0)
            high, low = split(jnp.concatenate([coeffs, swap_rows(coeffs)], axis=1))
            for i in range(1, per_far):
                near(s * per_far + i)
            both = dot(jnp.concatenate([high, low], axis=0), right_far[0, s])
            terms[n_near + s, :width] = fold(both) + dot(high, right_far[1, s])

        for s in range(n_far * step // STEPS, n_far * (step + 1) // STEPS):
            body(s)

    def make_sums(k):
        width, rows = plan.width[k], plan.rows(k)
        for j in list(range(1, n_dir)) + [0]:
            for i in range(n_row):
                q = row_of(i)
                target = c * n_row + lax.rem(d + j, n_dir) * per_dir + q // n_dir
                lanes = pl.ds(pl.multiple_of(lax.rem(q, n_dir) * piece, piece), piece)
                gains = [
                    jnp.where((near_pairs[1, s] == target) & (s < counts[0, 0]), 1.0, 0.0) for s in range(n_near)
                ] + [jnp.where((far_pairs[1, s] == target) & (s < counts[0, 1]), 1.0, 0.0) for s in range(n_far)]
                total = terms[0, :width, lanes] * gains[0]
                for s in range(1, n_near + n_far):
                    total = total + terms[s, :width, lanes] * gains[s]
                parts[j, i, rows] = total
                if j > 0 and plan.row_wide[k] < width:
                    send_part(k, j, i).start()
                if i == n_cross and plan.row_wide[k] > 0:
                    send_sum(k, i, j).start()
                if i < n_cross and plan.row_wide[k] > 0:

                    @pl.when(jnp.logical_not(gathers(i)))
                    def _():
                        send_pair(k, i, j).start()

    def add_part(k, step):
        rows = plan.dir_rows(k)
        for i in range(n_row * step // STEPS, n_row * (step + 1) // STEPS):
            total = parts[0, i, rows]
            for j in range(1, n_dir):
                send_part(k, j, i).wait_recv()
                total = total + dir_parts[j - 1, i, rows]
            parts[0, i, rows] = total
            if i == n_cross:
                send_row(k, i, r // 2).start()
            if i < n_cross:

                @pl.when(jnp.logical_not(gathers(i)))
                def _():
                    pair_part(k, i).start()

    def add_far(k, step):
        rows = plan.dir_rows(k)
        for i in range(n_row * step // STEPS, min(n_cross, n_row * (step + 1) // STEPS)):

            @pl.when(gathers(i))
            def _():
                pair_part(k, i).wait_recv()
                parts[0, i, rows] = parts[0, i, rows] + pair_dir[i, rows]
                send_row(k, i, r // 2).start()

    def add_pairs(k):
        rows, slots = plan.row_rows(k), plan.row_slots(k)
        for i in range(n_cross):

            @pl.when(gathers(i))
            def _():
                remote(
                    parts.at[:, i, rows], pair_in.at[i, :, slots], q_send.at[0], a_recv.at[k, i], row_peer(n_cross)
                ).wait_recv()
                for j in list(range(1, n_dir)) + [0]:
                    parts[j, i, rows] = parts[j, i, rows] + pair_in[i, j, slots]
                    send_sum(k, i, j).start()

    def add_rows(k):
        rows, slots = plan.row_rows(k), plan.row_slots(k)
        all_of = row_in.at[:, :, slots]
        remote(all_of, all_of, q_send.at[0], q_recv.at[k], row_peer(n_cross)).wait_recv()
        for j in list(range(1, n_dir)) + [0]:
            total = parts[j, own, rows]
            for p in range(n_row // 2):
                total = total + row_in[p, j, slots]
            parts[j, own, rows] = total
            if j > 0:
                send_last(k, j).start()

    def place(k, start, total):
        half, at = plan.half[k], plan.first[k]
        stop = start + total.shape[0]
        if start < half:
            cut = min(stop, half)
            totals[at + start : at + cut] = total[: cut - start]
        if stop > half:
            cut = max(start, half)
            base = wide // 2 + at - half
            totals[base + cut : base + stop] = total[cut - start :]

    def finish_dir(k):
        rows = plan.dir_rows(k)
        total = parts[0, own, rows]
        all_of = row_dir.at[:, rows]
        remote(all_of, all_of, r_send.at[0], r_recv.at[k], row_peer(n_cross)).wait_recv()
        for p in range(n_row // 2):
            total = total + row_dir[p, rows]
        place(k, 0, total)

    def finish_row(k):
        rows, slots = plan.row_rows(k), plan.row_slots(k)
        total = parts[0, own, rows]
        for j in range(1, n_dir):
            send_last(k, j).wait_recv()
            total = total + last_in[j - 1, slots]
        place(k, plan.width[k] - plan.row_wide[k], total)

    def put(first, last):
        for base in (0, wide // 2):
            columns = slice(base + first, base + last)
            out[:, columns] = totals[columns].T

    def drain():
        for j in range(1, n_dir):
            remote(sent, dir_in.at[j - 1], d_send.at[j - 1], d_recv.at[0, 0], dir_peer(1)).wait_send()
        for j in range(1, n_x):
            remote(gathered.at[0], gathered.at[0], x_send.at[j - 1], x_recv.at[0, 0], x_peer(1)).wait_send()
        all_of = gathered.at[pl.ds(0, n_x)]
        remote(all_of, all_of, c_send.at[0], c_recv.at[0], (d, r, partner)).wait_send()
        dir_rows, row_rows = pl.ds(0, plan.dir_total), pl.ds(0, sum(plan.row_wide))
        if plan.dir_total > 0:
            all_of = parts.at[pl.ds(1, n_dir - 1), :, dir_rows]
            remote(all_of, all_of, p_send.at[0], p_recv.at[0, 0, 0], dir_peer(1)).wait_send()
            all_of = parts.at[0, pl.ds(0, own), dir_rows]
            remote(all_of, all_of, r_send.at[0], r_recv.at[0], row_peer(n_cross)).wait_send()
        if sum(plan.row_wide) > 0:
            all_of = parts.at[:, pl.ds(0, own), row_rows]
            remote(all_of, all_of, q_send.at[0], q_recv.at[0], row_peer(n_cross)).wait_send()
            all_of = parts.at[pl.ds(1, n_dir - 1), own, row_rows]
            remote(all_of, all_of, l_send.at[0], l_recv.at[0, 0], dir_peer(1)).wait_send()

    inputs[0].wait()
    cot_t[...] = cot[...].T
    for load in inputs[1:]:
        load.wait()
    for item in range(stages):
        load_item(item).start()
    for s in range(min(2, n_far)):
        for load in load_far(s):
            load.start()
    early = next(k for k in range(chunks) if plan.first[k] + plan.half[k] >= 2 * wide // (2 * PARTS))
    for group in ((0, early), (early + 1, chunks - 1)):
        right_sides(*group)
        if group[0] == 0:
            pl.semaphore_wait(barrier, len(peers))
        for k in range(group[0], group[1] + 1):
            for u in plan.units_of(k):
                for j in range(1, n_dir):
                    send_dir(u, j).start()

    waiting = {k: (plan.row_wide[k] > 0) + (plan.row_wide[k] < plan.width[k]) for k in range(chunks)}
    put_at = [0]

    def finished(k):
        waiting[k] -= 1
        ends = [stop for stop in range(128, wide // 2 + 1, 128) if stop > put_at[0]]
        for stop in ends:
            if any(waiting[i] for i in range(chunks) if plan.first[i] < stop):
                return
            put(put_at[0], stop)
            put_at[0] = stop

    calls = {
        "convert": lambda i: convert(n_near * i // STEPS, n_near * (i + 1) // STEPS),
        "pack": pack_far,
        "dirs": add_dirs,
        "relay": relay,
        "sides": make_sides,
        "near": multiply,
        "sums": make_sums,
        "part": add_part,
        "far": add_far,
        "pairs": add_pairs,
        "rows": add_rows,
        "last": finish_dir,
        "end": finish_row,
    }
    for name, *at in ORDER:
        calls[name](*at)
        if name in ("last", "end"):
            finished(at[0])
    drain()


def shards(
    cotangent, radiation, near_z, near_pairs, far_ut, far_vt, far_pairs, far_ranks, block_counts
):
    n_dir, n_row, n_col = (lax.axis_size(name) for name in ("dir", "row", "col"))
    deep, wide = cotangent.shape
    small = n_row * n_col <= 16
    plan = Plan(wide, small)
    chunks, most = plan.chunks, max(plan.width)
    block = near_z.shape[2]
    n_near, n_far, rank_most = near_z.shape[1], far_ut.shape[1], far_ut.shape[2]
    n_x = n_col // CORES
    piece = block // n_dir
    stages = min(6 if small else 2, 2 * n_near)
    rank_pad = -(-rank_most // 128) * 128
    smem = pl.BlockSpec(memory_space=pltpu.SMEM)
    anywhere = pl.BlockSpec(memory_space=pl.ANY)
    dma = pltpu.SemaphoreType.DMA
    return pl.pallas_call(
        functools.partial(kernel, n_dir, n_row, n_col, plan),
        out_shape=pltpu.VMEM((piece, wide), F32),
        in_specs=[smem] * 4 + [anywhere] * 5,
        out_specs=pl.BlockSpec(memory_space=pltpu.VMEM),
        scratch_shapes=[
            pltpu.VMEM((deep, wide), BF16),
            pltpu.VMEM(radiation.shape, BF16),
            pltpu.VMEM((n_near, 2 * block, block), BF16),
            pltpu.VMEM((n_near, 2 * block, block), BF16),
            pltpu.VMEM((stages, block, block), F32),
            pltpu.VMEM((2, 4, rank_most, block), F32),
            pltpu.VMEM((n_far, 2 * block, 2 * rank_pad), BF16),
            pltpu.VMEM((2, n_far, 2 * rank_pad, block), BF16),
            pltpu.VMEM((wide, deep), BF16),
            pltpu.VMEM((wide, piece), F32),
            pltpu.VMEM((wide, block), F32),
            pltpu.VMEM((n_dir - 1, wide, block), F32),
            pltpu.VMEM((n_col, wide, block), F32),
            pltpu.VMEM((n_col, 2 * most, 2 * block), BF16),
            pltpu.VMEM((n_near + n_far, most, block), F32),
            pltpu.VMEM((n_dir, n_row, wide, piece), F32),
            pltpu.VMEM((n_dir - 1, n_row, wide, piece), F32),
            pltpu.VMEM((n_row - 2, wide, piece), F32),
            pltpu.VMEM((n_row // 2, wide, piece), F32),
            pltpu.VMEM((n_row - 2, n_dir, plan.row_total, piece), F32),
            pltpu.VMEM((n_row // 2, n_dir, plan.row_total, piece), F32),
            pltpu.VMEM((n_dir - 1, plan.row_total, piece), F32),
            dma((3,)),
            dma((stages,)),
            dma((2, 4)),
            dma((n_dir - 1,)),
            dma((sum(UNITS), n_dir - 1)),
            dma((n_x - 1,)),
            dma((sum(UNITS), n_x - 1)),
            dma((1,)),
            dma((chunks,)),
            dma((1,)),
            dma((chunks, n_dir - 1, n_row)),
            dma((1,)),
            dma((chunks, n_row - 2)),
            dma((chunks,)),
            dma((1,)),
            dma((chunks, n_row - 2)),
            dma((chunks,)),
            dma((1,)),
            dma((chunks, n_dir - 1)),
        ],
        compiler_params=pltpu.CompilerParams(
            collective_id=0, has_side_effects=True, vmem_limit_bytes=67043328 - 4 * piece * wide
        ),
    )(near_pairs.T, far_pairs.T, far_ranks, block_counts, cotangent, radiation, near_z, far_ut, far_vt)


def solution(mesh):
    return jax.shard_map(
        shards,
        mesh=mesh,
        in_specs=(
            P("dir", None),
            P(None, ("row", "col"), "dir"),
            P(None, ("dir", "row", "col"), None, None),
            P(("dir", "row", "col"), None),
            P(None, ("dir", "row", "col"), None, None),
            P(None, ("dir", "row", "col"), None, None),
            P(("dir", "row", "col"), None),
            P(("dir", "row", "col")),
            P(("dir", "row", "col"), None),
        ),
        out_specs=P(("col", "dir", "row"), None),
        check_vma=False,
    )
```
